128 devices in a mesh: span: 16 (over x, z), chord: 8 (over y, core).
Axes of the slice: x: 4, y: 4, z: 4, core: 2. Of those that a mesh axis runs over, the one named last changes fastest.
Arguments:
- fluid_state: float32 [4, 512, 256, 128], P(None, 'span', 'chord'), may hold values from -6 to 6
- shell_disp: float32 [3, 2048, 1024], P(None, 'span', 'chord'), may hold values from -6 to 6
- shell_vel: float32 [3, 2048, 1024], P(None, 'span', 'chord'), may hold values from -6 to 6
- owners: int32 [131072, 4], P(('span', 'chord')), may hold values from 0 to 127, all different within a row; in each aligned block of 1024 rows (0 to 1023, 1024 to 2047, ...) at most 64 rows name the same one
- node_local: int32 [131072, 4], P(('span', 'chord')), may hold values from 0 to 16383
- rbf_weight: float32 [131072, 4], P(('span', 'chord')), may hold values from 0.2 to 1
- normals: float32 [3, 131072], P(None, ('span', 'chord')), may hold values from -6 to 6
Outputs:
- fluid_next: float32 [4, 512, 256, 128], P(None, 'span', 'chord')
- interface_motion: float32 [6, 131072], P(None, ('span', 'chord'))
- disp_next: float32 [3, 2048, 1024], P(None, 'span', 'chord')
- vel_next: float32 [3, 2048, 1024], P(None, 'span', 'chord')
The draws below stay inside these ranges and needn't reach their ends.
Inputs may be any that keep to these rules, and one draw needn't show every extreme that they name: Each interface point names 4 different owners; the points of one device name no owner more than 64 times, a bound that some block reaches.
All inputs are finite; a program needn't handle non-finite values.
Results may differ from the reference program's by a relative error of at most 0.00007.
Values sent between devices are 32-bit elements; how exact they have to be, the bound alone decides.
A program may use at most 64 MiB of HBM per device.

```python
import math
import jax
import jax.numpy as jnp
import numpy as np
from jax import lax

CX = 32
CY = 32
SX = 128
SY = 128
K = 4
NX = 512
NY = 256
NZ = 128
SNX = 2048
SNY = 1024
POINTS = 131072
CAP = 64
N_SPAN = 16
N_CHORD = 8
DEVICES = 128


def plant(drawn, own_key, smallest, high):
    longest = drawn.shape.index(max(drawn.shape))
    spots = []
    for shift in (0, 1):
        where = [jax.random.randint(jax.random.fold_in(own_key, axis), (), 0, length) for axis, length in enumerate(drawn.shape)]
        where[longest] = (where[longest] + shift) % drawn.shape[longest]
        spots.append(tuple(where))
    return drawn.at[spots[0]].set(smallest).at[spots[1]].set(high)


def block_levels(rng, shape, pieces, smallest, high):
    def one(axis_at, shards_of):
        draws = jax.random.uniform(jax.random.fold_in(jax.random.fold_in(rng, 6), axis_at), (shards_of,), jnp.float32, smallest / len(pieces), high / len(pieces))
        return jnp.repeat(jnp.exp(draws), shape[axis_at] // shards_of).reshape((-1,) + (1,) * (len(shape) - axis_at - 1))

    level = one(*pieces[0])
    for cut in pieces[1:]:
        level = level * one(*cut)
    return level


def routed_block(stream_key, own, number, rows, count, top, reach, skew):
    sequence = jax.random.permutation(stream_key, count)
    packed, ordinary = load_shares(count, rows * top, reach, skew, True), load_shares(count, rows * top, reach, skew, False)
    places = jnp.arange(count)

    def named(sizes, turn):
        used = int((sizes > 0).sum())
        fixed = max(1, used // 4)
        passed = fixed + (places - fixed + turn * (used - fixed)) % max(1, count - fixed)
        return jnp.zeros((count,), jnp.int32).at[sequence[jnp.where(places < fixed, places, passed)]].set(jnp.asarray(sizes, jnp.int32))

    sizes = jnp.where(number % 4 == 0, named(packed, number // 4), named(ordinary, number - number // 4 - 1))
    mixed = jax.random.permutation(jax.random.fold_in(own, 3), count)
    giver, taker = mixed[0:count // 2 * 2:2], mixed[1:count // 2 * 2:2]
    slack = jnp.minimum(sizes[giver] - 1, reach - sizes[taker]) // 2
    slack = jnp.where((giver == sequence[0]) | (taker == sequence[0]) | (sizes[taker] == 0), 0, jnp.maximum(slack, 0))
    passed = jax.random.randint(jax.random.fold_in(own, 4), (count // 2,), 0, 1 << 20) % (slack + 1)
    sizes = sizes.at[giver].add(-passed).at[taker].add(passed)
    members = jnp.searchsorted(jnp.cumsum(sizes), jnp.arange(rows * top), side="right").astype(jnp.int32)
    grid = members.reshape(top, rows).T
    grid = grid[jax.random.permutation(jax.random.fold_in(own, 1), rows)]
    turn = jax.random.randint(jax.random.fold_in(own, 2), (rows, 1), 0, top)
    return jnp.take_along_axis(grid, (jnp.arange(top)[None, :] + turn) % top, axis=1)


def load_shares(amount, total, limit, skew, full):
    portions = [(1 << 20) // math.isqrt(rank ** skew) + 1 for rank in range(1, amount + 1)]
    largest = limit if full else min(limit, max(-(-total // amount), total * portions[0] // sum(portions)))
    least = 1 if total - largest >= amount - 1 else 0
    counts, spare = [largest] + [least] * (amount - 1), total - largest - least * (amount - 1)
    while spare > 0:
        movable = [i for i in range(1, amount) if counts[i] < largest] or [i for i in range(1, amount) if counts[i] < limit]
        whole, budget = sum([portions[i] for i in movable]), spare
        for i in movable:
            more = min(limit - counts[i], max(1, budget * portions[i] // whole), spare)
            counts[i] = counts[i] + more
            spare = spare - more
    return np.array(counts)


def normal_values(key, shape, width, bound, cuts=(), held_as=jnp.bfloat16):
    factor_of = block_levels(key, shape, cuts, -0.22, 0.18) if cuts else 1.0
    array = jax.random.normal(key, shape, jnp.float32) * width * factor_of
    return jnp.minimum(jnp.maximum(array, -bound), bound).astype(held_as)


def setup_inputs(seed: int = 0) -> dict:
    seeds = jax.random.split(jax.random.key(seed), 8)
    fluid_state = normal_values(seeds[0], (4, NX, NY, NZ), 1.0, 6.0, ((1, 16), (2, 8)), jnp.float32)
    shell_disp = normal_values(seeds[1], (3, SNX, SNY), 1.0, 6.0, ((1, 16), (2, 8)), jnp.float32)
    shell_vel = normal_values(seeds[2], (3, SNX, SNY), 1.0, 6.0, ((1, 16), (2, 8)), jnp.float32)
    owners_keys = jax.random.split(jax.random.fold_in(seeds[3], 1), POINTS // (CX * CY))
    owners_turns = jax.random.permutation(jax.random.fold_in(seeds[3], 3), POINTS // (CX * CY))
    owners = jax.vmap(lambda own, number: routed_block(jax.random.fold_in(seeds[3], 2), own, number, CX * CY, DEVICES, K, CAP, 2))(owners_keys, owners_turns).reshape((POINTS, K))
    node_local = plant(jax.random.randint(seeds[4], (POINTS, K), 0, SX * SY), jax.random.fold_in(seeds[4], 1), 0, (SX * SY) - 1).astype(jnp.int32)
    rbf_weight = jnp.clip(0.2 + 0.8 * jax.random.uniform(seeds[5], (POINTS, K), jnp.float32) ** block_levels(seeds[5], (POINTS, K), ((0, 128),), -0.2, 0.2), 0.2, 1.0)
    normals = normal_values(seeds[6], (3, POINTS), 1.0, 6.0, ((1, 128),), jnp.float32)
    return {"fluid_state": fluid_state, "shell_disp": shell_disp, "shell_vel": shell_vel, "owners": owners, "node_local": node_local, "rbf_weight": rbf_weight, "normals": normals}


flow_speed = 0.5
time_step = 0.4
stiffness = 0.5
damping = 0.2
shell_step = 0.3


def central(padded, direction):
    length = padded.shape[direction] - 6

    def window(offset):
        return lax.slice_in_dim(padded, 3 + offset, 3 + offset + length, axis=direction)

    return (45.0 * (window(1) - window(-1)) - 9.0 * (window(2) - window(-2)) + (window(3) - window(-3))) / 60.0


def wall_padded(fluid, wall_motion):
    mirror = fluid[:, :, :, 2::-1]
    moving = 2.0 * wall_motion[:, :, :, None] - mirror[1:]
    lower_ghost = jnp.concatenate([mirror[:1], moving], axis=0)
    upper_ghost = jnp.zeros(fluid.shape[:3] + (3,), fluid.dtype)
    return jnp.concatenate([lower_ghost, fluid, upper_ghost], axis=3)


def fluid_rates(span_padded, chord_padded, normal_padded):
    along_span = central(span_padded, 1)
    along_chord = central(chord_padded, 2)
    along_normal = central(normal_padded[0::3], 3)
    rate_p = -flow_speed * along_span[0] - (along_span[1] + along_chord[1] + along_normal[1])
    rate_u = -flow_speed * along_span[1] - along_span[0]
    rate_v = -flow_speed * along_span[2] - along_chord[0]
    rate_w = -flow_speed * along_span[3] - along_normal[0]
    return jnp.stack([rate_p, rate_u, rate_v, rate_w])


def laplacian(padded):
    center = padded[:, 1:-1, 1:-1]
    return padded[:, 2:, 1:-1] + padded[:, :-2, 1:-1] + padded[:, 1:-1, 2:] + padded[:, 1:-1, :-2] - 4.0 * center


def reference(fluid_state, shell_disp, shell_vel, owners, node_local, rbf_weight, normals):
    points = jnp.arange(CX * CY * N_SPAN * N_CHORD, dtype=jnp.int32)
    owner_block = points // (CX * CY)
    inside = points % (CX * CY)
    point_x = (owner_block // N_CHORD) * CX + inside // CY
    point_y = (owner_block % N_CHORD) * CY + inside % CY
    node_x = (owners // N_CHORD) * SX + node_local // SY
    node_y = (owners % N_CHORD) * SY + node_local % SY
    stacked = jnp.concatenate([shell_disp, shell_vel], axis=0)
    motion = stacked[:, node_x, node_y]
    interface_motion = jnp.sum(motion * rbf_weight[None], axis=2)
    wall_motion = jnp.zeros((3, CX * N_SPAN, CY * N_CHORD), jnp.float32).at[:, point_x, point_y].set(interface_motion[3:])
    span_padded = jnp.pad(fluid_state, ((0, 0), (3, 3), (0, 0), (0, 0)))
    chord_padded = jnp.pad(fluid_state[0::2], ((0, 0), (0, 0), (3, 3), (0, 0)))
    normal_padded = wall_padded(fluid_state, wall_motion)
    fluid_next = fluid_state + time_step * fluid_rates(span_padded, chord_padded, normal_padded)
    pressure = fluid_next[0, point_x, point_y, 0]
    surface_load = normals * pressure[None]
    contrib = surface_load[:, :, None] * rbf_weight[None]
    shell_force = jnp.zeros((3, SX * N_SPAN, SY * N_CHORD), jnp.float32).at[:, node_x, node_y].add(contrib)
    bending = laplacian(jnp.pad(shell_disp, ((0, 0), (1, 1), (1, 1))))
    acceleration = stiffness * bending + shell_force - damping * shell_vel
    vel_next = shell_vel + shell_step * acceleration
    disp_next = shell_disp + shell_step * vel_next
    return fluid_next, interface_motion, disp_next, vel_next
```

```python
import jax
import jax.numpy as jnp
from jax import lax
from jax.experimental import pallas as pl
from jax.experimental.pallas import tpu as pltpu
from jax.sharding import PartitionSpec as P

MESH = pl.DeviceIdType.MESH
F32, BF16, I32 = jnp.float32, jnp.bfloat16, jnp.int32
NS, NC, ND = 16, 8, 128
CAP = 64
CX, CY, NZ = 32, 32, 128
PTS, K = 1024, 4
ENT = PTS * K
SLOTS = ND * CAP
QW = 256
SCALE = 0.4 / 60.0
NT = (((1,), (1,)), ((), ()))


def iota(shape, dim):
    return lax.broadcasted_iota(I32, shape, dim)


def split(value):
    high = value.astype(BF16)
    return high, (value - high.astype(F32)).astype(BF16)


def dot(a, b):
    return jnp.dot(a, b, preferred_element_type=F32)


def dot_nt(a, b):
    return lax.dot_general(a, b, NT, preferred_element_type=F32)


def diff(far_up, mid_up, up, down, mid_down, far_down):
    return 45.0 * (up - down) - 9.0 * (mid_up - mid_down) + (far_up - far_down)


def stencil(distance):
    size = jnp.abs(distance)
    value = jnp.where(size == 1, 45.0, jnp.where(size == 2, -9.0, jnp.where(size == 3, 1.0, 0.0)))
    return jnp.where(distance > 0, value, -value)


def kernel(
    own_ref, node_ref, w_ref, nrm_ref, fluid_hbm, disp_hbm, vel_hbm,
    fluid_out, motion_ref, disp_out, vel_out,
    xbuf, ybuf, fo, zb, dbuf, vbuf,
    onehot, rank, reqb, req, asked, px, py,
    table, ohy, ohx, picked, rep, got, lookup, p0,
    loadb, outg, arrived, vals, fb, force, colsend, collow, colhigh,
    in_sem, out_sem, halo_s, halo_r, a2a_s, a2a_r,
):
    span, chord = lax.axis_index("span"), lax.axis_index("chord")
    me = span * NC + chord

    def place(p):
        return (p // NC, lax.rem(p, NC))

    loads = [
        pltpu.make_async_copy(disp_hbm, dbuf.at[:, pl.ds(8, 128)], in_sem.at[0]),
        pltpu.make_async_copy(vel_hbm, vbuf, in_sem.at[1]),
        pltpu.make_async_copy(fluid_hbm, xbuf.at[:, pl.ds(3, CX)], in_sem.at[2]),
        pltpu.make_async_copy(fluid_hbm.at[0], ybuf.at[0, :, pl.ds(8, CY)], in_sem.at[3]),
        pltpu.make_async_copy(fluid_hbm.at[2], ybuf.at[1, :, pl.ds(8, CY)], in_sem.at[4]),
    ]
    for c in loads:
        c.start()

    barrier = pltpu.get_barrier_semaphore()

    def greet(d, carry):
        pl.semaphore_signal(barrier, 1, device_id=place(lax.rem(me + d, ND)), device_id_type=MESH)
        return carry

    lax.fori_loop(1, ND, greet, 0)

    before = (iota((QW, QW), 0) < iota((QW, QW), 1)).astype(F32).astype(BF16)
    ones = jnp.ones((QW, QW), BF16)
    sub_o = iota((ND, QW), 0)
    sub_s = iota((CAP, QW), 0)
    offset = jnp.zeros((ND, QW), F32)
    for q in range(PTS // QW):
        cols = slice(q * QW, (q + 1) * QW)
        masks = []
        count = jnp.zeros((ND, QW), F32)
        for k in range(K):
            mask = sub_o == own_ref[k : k + 1, cols]
            masks.append(mask)
            hot = jnp.where(mask, 1.0, 0.0)
            onehot[:, k * PTS + q * QW : k * PTS + (q + 1) * QW] = hot.astype(BF16)
            count = count + hot
        count = count.astype(BF16)
        prior = dot(count, before) + offset
        offset = offset + dot(count, ones)
        for k in range(K):
            slot = jnp.sum(jnp.where(masks[k], prior, 0.0), axis=0, keepdims=True).astype(I32)
            rank[k : k + 1, cols] = slot
            node = node_ref[k : k + 1, cols]
            at = sub_s == slot
            ent = slice(k * PTS + q * QW, k * PTS + (q + 1) * QW)
            reqb[0:CAP, ent] = jnp.where(at, (node // 128).astype(F32), 0.0).astype(BF16)
            reqb[CAP:, ent] = jnp.where(at, lax.rem(node, 128).astype(F32), 0.0).astype(BF16)
    req[0] = dot_nt(onehot[...], reqb[...])

    pl.semaphore_wait(barrier, ND - 1)

    def exchange(src, dst, index):
        def send(d, carry):
            p = lax.rem(me + d, ND)
            pltpu.make_async_remote_copy(
                src.at[:, pl.ds(p, 1)], dst.at[:, pl.ds(me, 1)], a2a_s.at[index], a2a_r.at[index],
                device_id=place(p), device_id_type=MESH,
            ).start()
            return carry

        lax.fori_loop(1, ND, send, 0)
        dst[:, pl.ds(me, 1), :] = src[:, pl.ds(me, 1), :]

    def whole(src, dst, index):
        return pltpu.make_async_remote_copy(
            src.at[:, pl.ds(0, ND - 1)], dst.at[:, pl.ds(0, ND - 1)], a2a_s.at[index], a2a_r.at[index],
            device_id=place(me), device_id_type=MESH,
        )

    exchange(req, asked, 0)

    for c in loads:
        c.wait()
    for c in range(3):
        turned = dbuf[c, 8:136, :].T
        colsend[0, c : c + 1, :] = turned[0:1, :]
        colsend[1, c : c + 1, :] = turned[127:128, :]
    up = (lax.rem(span + 1, NS), chord)
    down = (lax.rem(span + NS - 1, NS), chord)
    right = (span, lax.rem(chord + 1, NC))
    left = (span, lax.rem(chord + NC - 1, NC))
    moves = [
        (xbuf.at[:, pl.ds(CX, 3)], xbuf.at[:, pl.ds(0, 3)], up),
        (xbuf.at[:, pl.ds(3, 3)], xbuf.at[:, pl.ds(CX + 3, 3)], down),
        (ybuf.at[:, :, pl.ds(CY + 5, 3)], ybuf.at[:, :, pl.ds(5, 3)], right),
        (ybuf.at[:, :, pl.ds(8, 3)], ybuf.at[:, :, pl.ds(CY + 8, 3)], left),
        (dbuf.at[:, pl.ds(135, 1)], dbuf.at[:, pl.ds(7, 1)], up),
        (dbuf.at[:, pl.ds(8, 1)], dbuf.at[:, pl.ds(136, 1)], down),
        (colsend.at[1], collow, right),
        (colsend.at[0], colhigh, left),
    ]
    halos = [
        pltpu.make_async_remote_copy(a, b, halo_s.at[i], halo_r.at[i], device_id=to, device_id_type=MESH)
        for i, (a, b, to) in enumerate(moves)
    ]
    for h in halos:
        h.start()

    for c in range(6):
        value = dbuf[c, 8:136, :] if c < 3 else vbuf[c - 3]
        high, low = split(value)
        table[c * 128 : (c + 1) * 128, 0:128] = high
        table[c * 128 : (c + 1) * 128, 128:256] = low

    src, tgt = iota((NZ, NZ), 0), iota((NZ, NZ), 1)
    inner = stencil(src - tgt)
    ghost = jnp.where(src < 3, stencil(-(src + 1 + tgt)), 0.0)
    for i, (f, tab) in enumerate(((0, inner + ghost), (3, inner - ghost))):
        tab = tab.astype(BF16)
        tab = jnp.concatenate([tab, tab], axis=0)
        for b in range(4):
            high, low = split(xbuf[f, 3 + 8 * b : 11 + 8 * b].reshape(256, NZ))
            zb[i, b * 256 : (b + 1) * 256, :] = dot(jnp.concatenate([high, low], axis=1), tab)

    first = whole(req, asked, 0)
    first.wait_recv()
    lane = iota((CAP, 128), 1)
    a, b = asked[0, 0:64, :], asked[0, 64:128, :]
    ar, br = pltpu.roll(a, 64, 1), pltpu.roll(b, 64, 1)
    px[...] = jnp.where(lane < 64, a, br).astype(I32)
    py[...] = jnp.where(lane < 64, ar, b).astype(I32)

    lane8 = iota((8, 128), 1)

    def pick(g0, carry):
        g = lax.rem(g0 + span, 8)
        rows = pl.ds(pl.multiple_of(g * 8, 8), 8)
        xs, ys = px[rows, :], py[rows, :]
        for t in range(4):
            yrow = jnp.concatenate([ys[2 * t : 2 * t + 1], ys[2 * t + 1 : 2 * t + 2]], axis=1)
            xrow = jnp.concatenate([xs[2 * t : 2 * t + 1], xs[2 * t + 1 : 2 * t + 2]], axis=1)
            hot = jnp.where(sub_o == yrow, 1.0, 0.0).astype(BF16)
            ohy[:, pl.ds(pl.multiple_of((g * 4 + t) * QW, QW), QW)] = hot
            out = dot(table[...], jnp.concatenate([hot, hot], axis=0))
            mask = sub_o == xrow
            for c in range(6):
                row = jnp.sum(jnp.where(mask, out[c * 128 : (c + 1) * 128], 0.0), axis=0, keepdims=True)
                picked[c, 2 * t : 2 * t + 1, :] = row[:, 0:128]
                picked[c, 2 * t + 1 : 2 * t + 2, :] = row[:, 128:256]
        high_rows = pl.ds(pl.multiple_of(g * 8 + 64, 8), 8)
        for j in range(3):
            even, odd = picked[2 * j], picked[2 * j + 1]
            rep[j, rows, :] = jnp.where(lane8 < 64, even, pltpu.roll(odd, 64, 1))
            rep[j, high_rows, :] = jnp.where(lane8 < 64, pltpu.roll(even, 64, 1), odd)

        def reply(i, inner_carry):
            p = g * 8 + lax.rem(i, 8) + (i // 8) * 64

            @pl.when(p != me)
            def _():
                pltpu.make_async_remote_copy(
                    rep.at[:, pl.ds(p, 1)], got.at[:, pl.ds(me, 1)], a2a_s.at[1], a2a_r.at[1],
                    device_id=place(p), device_id_type=MESH,
                ).start()

            return inner_carry

        lax.fori_loop(0, 16, reply, 0)
        return carry

    lax.fori_loop(0, 8, pick, 0)
    got[:, pl.ds(me, 1), :] = rep[:, pl.ds(me, 1), :]

    for h in halos:
        h.wait_recv()

    @pl.when(span == 0)
    def _():
        xbuf[:, 0:3] = jnp.zeros((4, 3, CY, NZ), F32)
        dbuf[:, 7:8, :] = jnp.zeros((3, 1, 128), F32)

    @pl.when(span == NS - 1)
    def _():
        xbuf[:, CX + 3 : CX + 6] = jnp.zeros((4, 3, CY, NZ), F32)
        dbuf[:, 136:137, :] = jnp.zeros((3, 1, 128), F32)

    @pl.when(chord == 0)
    def _():
        ybuf[:, :, 5:8, :] = jnp.zeros((2, CX, 3, NZ), F32)
        collow[...] = jnp.zeros((8, 128), F32)

    @pl.when(chord == NC - 1)
    def _():
        ybuf[:, :, CY + 8 : CY + 11, :] = jnp.zeros((2, CX, 3, NZ), F32)
        colhigh[...] = jnp.zeros((8, 128), F32)

    def plane(x, carry):
        def dx(f):
            return diff(*[xbuf[f, x + 3 + o] for o in (3, 2, 1, -1, -2, -3)])

        def dy(f):
            return diff(*[ybuf[f, x, 8 + o : 8 + CY + o, :] for o in (3, 2, 1, -1, -2, -3)])

        zrows = pl.ds(pl.multiple_of(x * CY, CY), CY)
        dp, du = dx(0), dx(1)
        fo[0, x] = xbuf[0, x + 3] - SCALE * (0.5 * dp + du + dy(1) + zb[1, zrows, :])
        fo[1, x] = xbuf[1, x + 3] - SCALE * (0.5 * du + dp)
        fo[2, x] = xbuf[2, x + 3] - SCALE * (0.5 * dx(2) + dy(0))
        fo[3, x] = xbuf[3, x + 3] - SCALE * (0.5 * dx(3) + zb[0, zrows, :])
        return carry

    lax.fori_loop(0, CX, plane, 0)
    flow_out = pltpu.make_async_copy(fo.at[pl.ds(1, 3)], fluid_out.at[pl.ds(1, 3)], out_sem.at[0])
    flow_out.start()
    for b in range(8):
        turned = fo[0, 4 * b : 4 * b + 4].reshape(128, NZ).T
        p0[0:1, b * 128 : (b + 1) * 128] = turned[0:1, :]

    def columns(g, carry):
        rows = pl.ds(pl.multiple_of(g * 8, 8), 8)
        xs = px[rows, :]
        for t in range(8):
            hot = jnp.where(sub_o[:, 0:128] == xs[t : t + 1], 1.0, 0.0).astype(BF16)
            ohx[:, pl.ds(pl.multiple_of((g * 8 + t) * 128, 128), 128)] = hot
        return carry

    lax.fori_loop(0, 8, columns, 0)

    second = whole(rep, got, 1)
    second.wait_recv()
    for j in range(3):
        high, low = split(got[j].T)
        lookup[j * 128 : (j + 1) * 128, 0:128] = high
        lookup[j * 128 : (j + 1) * 128, 128:256] = low

    def interp(q, carry):
        cols = pl.ds(pl.multiple_of(q * QW, QW), QW)
        totals = [jnp.zeros((8, QW), F32) for _ in range(6)]
        for k in range(K):
            hot = onehot[:, pl.ds(pl.multiple_of(k * PTS + q * QW, QW), QW)]
            out = dot(lookup[...], jnp.concatenate([hot, hot], axis=0))
            at = sub_s == rank[k : k + 1, cols]
            weight = w_ref[k : k + 1, cols]
            for c in range(6):
                part = jnp.where(at, out[c * CAP : (c + 1) * CAP], 0.0)
                totals[c] = totals[c] + weight * jnp.sum(part.reshape(8, 8, QW), axis=0)
        for c in range(6):
            motion_ref[c : c + 1, cols] = jnp.sum(totals[c], axis=0, keepdims=True)
        return carry

    lax.fori_loop(0, PTS // QW, interp, 0)

    pressure = p0[0:1, :] + (SCALE * 74.0) * motion_ref[5:6, :]
    for q in range(PTS // QW):
        cols = slice(q * QW, (q + 1) * QW)
        for k in range(K):
            ent = slice(k * PTS + q * QW, k * PTS + (q + 1) * QW)
            at = sub_s == rank[k : k + 1, cols]
            for c in range(3):
                value = nrm_ref[c : c + 1, cols] * pressure[:, cols] * w_ref[k : k + 1, cols]
                high = value.astype(BF16).astype(F32)
                loadb[c * CAP : (c + 1) * CAP, ent] = jnp.where(at, high, 0.0).astype(BF16)
                loadb[256 + c * CAP : 256 + (c + 1) * CAP, ent] = jnp.where(at, value - high, 0.0).astype(BF16)
    loadb[192:256, :] = jnp.zeros((64, ENT), BF16)
    loadb[448:512, :] = jnp.zeros((64, ENT), BF16)
    both = dot_nt(onehot[...], loadb[...])
    outg[0] = both[:, 0:128] + both[:, 256:384]
    outg[1] = both[:, 128:256] + both[:, 384:512]
    exchange(outg, arrived, 2)

    zlane = iota((128, NZ), 1)
    reach = jnp.where(zlane == 0, 74.0 * SCALE, jnp.where(zlane == 1, -16.0 * SCALE, jnp.where(zlane == 2, 2.0 * SCALE, 0.0)))
    for b in range(8):
        turned = jnp.broadcast_to(motion_ref[5:6, b * 128 : (b + 1) * 128], (8, 128)).T
        fix = (turned[:, 0:1] * reach).reshape(4, CY, NZ)
        fo[0, 4 * b : 4 * b + 4] = fo[0, 4 * b : 4 * b + 4] + fix
    pressure_out = pltpu.make_async_copy(fo.at[0], fluid_out.at[0], out_sem.at[1])
    pressure_out.start()

    third = whole(outg, arrived, 2)
    third.wait_recv()
    for c, j in ((0, 0), (1, 0), (2, 1)):
        a, b = arrived[j, 0:64, :], arrived[j, 64:128, :]
        if c == 1:
            value = jnp.where(lane < 64, pltpu.roll(a, 64, 1), b)
        else:
            value = jnp.where(lane < 64, a, pltpu.roll(b, 64, 1))
        high = value.astype(BF16).astype(F32)
        vals[c] = high
        vals[3 + c] = value - high
    force[...] = jnp.zeros((384, 128), F32)

    def collect(g, carry):
        rows = pl.ds(pl.multiple_of(g * 8, 8), 8)
        cols = pl.ds(pl.multiple_of(g * 1024, 1024), 1024)
        for half in range(2):
            for c in range(3):
                value = vals[half * 3 + c, rows, :]
                for t in range(8):
                    spread = jnp.broadcast_to(value[t : t + 1], (16, 128)).astype(BF16)
                    spread = jnp.concatenate([spread] * 8, axis=0)
                    hot = ohx[:, pl.ds(pl.multiple_of((g * 8 + t) * 128, 128), 128)]
                    fb[c * 128 : (c + 1) * 128, half * 1024 + t * 128 : half * 1024 + (t + 1) * 128] = hot * spread
        hoty = ohy[:, cols]
        force[...] += dot_nt(fb[...], jnp.concatenate([hoty, hoty], axis=1))
        return carry

    lax.fori_loop(0, 8, collect, 0)

    lane128 = iota((128, 128), 1)
    low_t, high_t = collow[...].T, colhigh[...].T
    for c in range(3):
        mid = dbuf[c, 8:136, :]
        west = jnp.where(lane128 == 0, low_t[:, c : c + 1], pltpu.roll(mid, 1, 1))
        east = jnp.where(lane128 == 127, high_t[:, c : c + 1], pltpu.roll(mid, 127, 1))
        lap = dbuf[c, 9:137, :] + dbuf[c, 7:135, :] + east + west - 4.0 * mid
        vel = vbuf[c]
        vel_new = vel + 0.3 * (0.5 * lap + force[c * 128 : (c + 1) * 128, :] - 0.2 * vel)
        vel_out[c] = vel_new
        disp_out[c] = mid + 0.3 * vel_new

    for h in halos:
        h.wait_send()
    first.wait_send()
    second.wait_send()
    third.wait_send()
    flow_out.wait()
    pressure_out.wait()


def body(fluid, disp, vel, owners, nodes, weights, normals):
    small = pl.BlockSpec(memory_space=pltpu.VMEM)
    big = pl.BlockSpec(memory_space=pl.ANY)
    vm = pltpu.VMEM
    dma = pltpu.SemaphoreType.DMA
    scratch = [
        vm((4, CX + 6, CY, NZ), F32),
        vm((2, CX, CY + 16, NZ), F32),
        vm((4, CX, CY, NZ), F32),
        vm((2, PTS, NZ), F32),
        vm((3, 144, 128), F32),
        vm((3, 128, 128), F32),
        vm((ND, ENT), BF16),
        vm((K, PTS), I32),
        vm((128, ENT), BF16),
        vm((1, ND, 128), F32),
        vm((1, ND, 128), F32),
        vm((CAP, 128), I32),
        vm((CAP, 128), I32),
        vm((768, 256), BF16),
        vm((128, SLOTS), BF16),
        vm((128, SLOTS), BF16),
        vm((6, 8, 128), F32),
        vm((3, ND, 128), F32),
        vm((3, ND, 128), F32),
        vm((384, 256), BF16),
        vm((8, PTS), F32),
        vm((512, ENT), BF16),
        vm((2, ND, 128), F32),
        vm((2, ND, 128), F32),
        vm((6, CAP, 128), F32),
        vm((384, 2048), BF16),
        vm((384, 128), F32),
        vm((2, 8, 128), F32),
        vm((8, 128), F32),
        vm((8, 128), F32),
        dma((5,)),
        dma((2,)),
        dma((8,)),
        dma((8,)),
        dma((3,)),
        dma((3,)),
    ]
    return pl.pallas_call(
        kernel,
        name="coupling",
        out_shape=(
            jax.ShapeDtypeStruct(fluid.shape, F32),
            jax.ShapeDtypeStruct((6, PTS), F32),
            jax.ShapeDtypeStruct(disp.shape, F32),
            jax.ShapeDtypeStruct(vel.shape, F32),
        ),
        in_specs=[small] * 4 + [big] * 3,
        out_specs=(big, small, small, small),
        scratch_shapes=scratch,
        compiler_params=pltpu.CompilerParams(
            collective_id=0, has_side_effects=True, vmem_limit_bytes=56 * 1024 * 1024
        ),
    )(owners.T, nodes.T, weights.T, normals, fluid, disp, vel)


def solution(mesh):
    block, line = P(None, "span", "chord"), P(("span", "chord"), None)
    return jax.shard_map(
        body,
        mesh=mesh,
        in_specs=(P(None, "span", "chord", None), block, block, line, line, line, P(None, ("span", "chord"))),
        out_specs=(P(None, "span", "chord", None), P(None, ("span", "chord")), block, block),
        check_vma=False,
    )
```

```python
import jax
import jax.numpy as jnp
from jax import lax
from jax.experimental import pallas as pl
from jax.experimental.pallas import tpu as pltpu
from jax.sharding import PartitionSpec as P

MESH = pl.DeviceIdType.MESH
F32, BF16, I32 = jnp.float32, jnp.bfloat16, jnp.int32
NS, NC, ND = 16, 8, 128
CAP = 64
CX, CY, NZ = 32, 32, 128
PTS, K = 1024, 4
ENT = PTS * K
SLOTS = ND * CAP
QW = 256
SCALE = 0.4 / 60.0
NT = (((1,), (1,)), ((), ()))


def iota(shape, dim):
    return lax.broadcasted_iota(I32, shape, dim)


def split(value):
    high = value.astype(BF16)
    return high, (value - high.astype(F32)).astype(BF16)


def dot(a, b):
    return jnp.dot(a, b, preferred_element_type=F32)


def dot_nt(a, b):
    return lax.dot_general(a, b, NT, preferred_element_type=F32)


def diff(far_up, mid_up, up, down, mid_down, far_down):
    return 45.0 * (up - down) - 9.0 * (mid_up - mid_down) + (far_up - far_down)


def stencil(distance):
    size = jnp.abs(distance)
    value = jnp.where(size == 1, 45.0, jnp.where(size == 2, -9.0, jnp.where(size == 3, 1.0, 0.0)))
    return jnp.where(distance > 0, value, -value)


def kernel(
    own_ref, node_ref, w_ref, nrm_ref, fluid_hbm, disp_hbm, vel_hbm,
    fo, motion_ref, disp_out, vel_out,
    xbuf, ybuf, zb, dbuf, vbuf,
    onehot, rank, reqb, req, asked, px,
    table, ohy, ohx, picked, rep, got, lookup, p0,
    loadb, outg, arrived, fb, force, spread, colsend, collow, colhigh,
    in_sem, halo_s, halo_r, sent, ask_r, reply_r, load_r,
):
    span, chord = lax.axis_index("span"), lax.axis_index("chord")
    me = span * NC + chord

    mine = span // 2
    slot_row = mine * 8 + chord + 64 * lax.rem(span, 2)

    loads = [
        pltpu.make_async_copy(disp_hbm, dbuf.at[:, pl.ds(8, 128)], in_sem.at[0]),
        pltpu.make_async_copy(vel_hbm, vbuf, in_sem.at[1]),
        pltpu.make_async_copy(fluid_hbm, xbuf.at[:, pl.ds(3, CX)], in_sem.at[2]),
        pltpu.make_async_copy(fluid_hbm.at[0], ybuf.at[0, :, pl.ds(8, CY)], in_sem.at[3]),
        pltpu.make_async_copy(fluid_hbm.at[2], ybuf.at[1, :, pl.ds(8, CY)], in_sem.at[4]),
    ]
    for c in loads:
        c.start()

    barrier = pltpu.get_barrier_semaphore()

    def far_first(k):
        half = (k + 1) // 2
        return lax.rem(span + 10 + jnp.where(lax.rem(k, 2) == 1, half, 16 - half), NS)

    def each_peer(act):
        def one(k, carry):
            s = far_first(k)

            @pl.when(s != span)
            def _():
                for c in range(NC):
                    act(s, c)

            return carry

        lax.fori_loop(0, NS, one, 0)
        for c in range(NC):

            @pl.when(c != chord)
            def _():
                act(span, c)

    each_peer(lambda s, c: pl.semaphore_signal(barrier, 1, device_id=(s, c), device_id_type=MESH))

    before = (iota((QW, QW), 0) < iota((QW, QW), 1)).astype(F32).astype(BF16)
    ones = jnp.ones((QW, QW), BF16)
    sub_o = iota((ND, QW), 0)
    sub_s = iota((CAP, QW), 0)
    offset = jnp.zeros((ND, QW), F32)
    for q in range(PTS // QW):
        cols = slice(q * QW, (q + 1) * QW)
        masks = []
        count = jnp.zeros((ND, QW), F32)
        for k in range(K):
            mask = sub_o == own_ref[k : k + 1, cols]
            masks.append(mask)
            hot = jnp.where(mask, 1.0, 0.0)
            onehot[:, k * PTS + q * QW : k * PTS + (q + 1) * QW] = hot.astype(BF16)
            count = count + hot
        count = count.astype(BF16)
        prior = dot(count, before) + offset
        offset = offset + dot(count, ones)
        for k in range(K):
            slot = jnp.sum(jnp.where(masks[k], prior, 0.0), axis=0, keepdims=True).astype(I32)
            rank[k : k + 1, cols] = slot
            node = node_ref[k : k + 1, cols]
            at = sub_s == slot
            ent = slice(k * PTS + q * QW, k * PTS + (q + 1) * QW)
            reqb[0:CAP, ent] = jnp.where(at, (node // 256).astype(F32), 0.0).astype(BF16)
            reqb[CAP:, ent] = jnp.where(at, lax.rem(node, 256).astype(F32), 0.0).astype(BF16)
    req[0] = dot_nt(onehot[...], reqb[...])

    for c in loads:
        c.wait()
    for c in range(6):
        for odd in range(2):
            value = dbuf[c, pl.ds(8 + odd, 64, stride=2), :] if c < 3 else vbuf[c - 3, pl.ds(odd, 64, stride=2), :]
            high, low = split(value)
            for t in range(4):
                rows = slice(t * 96 + c * 16, t * 96 + (c + 1) * 16)
                table[rows, odd * 128 : (odd + 1) * 128] = high[t * 16 : (t + 1) * 16]
                table[rows, 256 + odd * 128 : 256 + (odd + 1) * 128] = low[t * 16 : (t + 1) * 16]
    for c in range(3):
        turned = dbuf[c, 8:136, :].T
        colsend[0, c : c + 1, :] = turned[0:1, :]
        colsend[1, c : c + 1, :] = turned[127:128, :]
    loadb[192:256, :] = jnp.zeros((64, ENT), BF16)
    loadb[448:512, :] = jnp.zeros((64, ENT), BF16)
    force[...] = jnp.zeros((384, 256), F32)

    src, tgt = iota((NZ, NZ), 0), iota((NZ, NZ), 1)
    inner = stencil(src - tgt)
    ghost = jnp.where(src < 3, stencil(-(src + 1 + tgt)), 0.0)
    for i, (f, tab) in enumerate(((0, inner + ghost), (3, inner - ghost))):
        tab = tab.astype(BF16)
        tab = jnp.concatenate([tab, tab], axis=0)
        for b in range(4):
            high, low = split(xbuf[f, 3 + 8 * b : 11 + 8 * b].reshape(256, NZ))
            zb[i, b * 256 : (b + 1) * 256, :] = dot(jnp.concatenate([high, low], axis=1), tab)

    pl.semaphore_wait(barrier, ND - 1)

    def row(ref, at):
        return ref.at[:, pl.ds(at, 1)]

    def exchange(src, dst, index, recv):
        def send(s, c):
            pltpu.make_async_remote_copy(
                row(src, s * NC + c), row(dst, slot_row), sent.at[index], recv.at[mine],
                device_id=(s, c), device_id_type=MESH,
            ).start()

        each_peer(send)
        dst[:, pl.ds(slot_row, 1), :] = src[:, pl.ds(me, 1), :]

    def some(src, dst, count, send_sem, recv_sem):
        return pltpu.make_async_remote_copy(
            src.at[:, pl.ds(0, count)], dst.at[:, pl.ds(0, count)], send_sem, recv_sem,
            device_id=(span, chord), device_id_type=MESH,
        )

    def await_group(src, dst, index, recv, g):
        @pl.when(g == mine)
        def _():
            some(src, dst, 15, sent.at[index], recv.at[g]).wait_recv()

        @pl.when(g != mine)
        def _():
            some(src, dst, 16, sent.at[index], recv.at[g]).wait_recv()

    def near_first(k):
        half = (k + 1) // 2
        return lax.rem(mine + jnp.where(lax.rem(k, 2) == 1, half, 8 - half), 8)

    exchange(req, asked, 0, ask_r)

    up = (lax.rem(span + 1, NS), chord)
    down = (lax.rem(span + NS - 1, NS), chord)
    right = (span, lax.rem(chord + 1, NC))
    left = (span, lax.rem(chord + NC - 1, NC))
    moves = [
        (xbuf.at[:, pl.ds(CX, 3)], xbuf.at[:, pl.ds(0, 3)], up),
        (xbuf.at[:, pl.ds(3, 3)], xbuf.at[:, pl.ds(CX + 3, 3)], down),
        (ybuf.at[:, :, pl.ds(CY + 5, 3)], ybuf.at[:, :, pl.ds(5, 3)], right),
        (ybuf.at[:, :, pl.ds(8, 3)], ybuf.at[:, :, pl.ds(CY + 8, 3)], left),
        (dbuf.at[:, pl.ds(135, 1)], dbuf.at[:, pl.ds(7, 1)], up),
        (dbuf.at[:, pl.ds(8, 1)], dbuf.at[:, pl.ds(136, 1)], down),
        (colsend.at[1], collow, right),
        (colsend.at[0], colhigh, left),
    ]
    halos = [
        pltpu.make_async_remote_copy(a, b, halo_s.at[i], halo_r.at[i], device_id=to, device_id_type=MESH)
        for i, (a, b, to) in enumerate(moves)
    ]
    for h in halos:
        h.start()

    lane8 = iota((8, 128), 1)
    sub8 = iota((8, QW), 0)
    sub_y = iota((QW, QW), 0)

    def halves(ref, j, g):
        low = ref[j, pl.ds(pl.multiple_of(g * 8, 8), 8), :]
        high = ref[j, pl.ds(pl.multiple_of(g * 8 + 64, 8), 8), :]
        front = jnp.where(lane8 < 64, low, pltpu.roll(high, 64, 1))
        back = jnp.where(lane8 < 64, pltpu.roll(low, 64, 1), high)
        return front, back

    def pick(k, carry):
        g = near_first(k)
        await_group(req, asked, 0, ask_r, g)
        rows = pl.ds(pl.multiple_of(g * 8, 8), 8)
        xs, ys = halves(asked, 0, g)
        xs, ys = xs.astype(I32), ys.astype(I32)
        px[rows, :] = xs
        for t in range(4):
            yrow = jnp.concatenate([ys[2 * t : 2 * t + 1], ys[2 * t + 1 : 2 * t + 2]], axis=1)
            xrow = jnp.concatenate([xs[2 * t : 2 * t + 1], xs[2 * t + 1 : 2 * t + 2]], axis=1)
            hot = jnp.where(sub_y == yrow, 1.0, 0.0).astype(BF16)
            ohy[:, pl.ds(pl.multiple_of((g * 4 + t) * QW, QW), QW)] = hot
            out = dot(table[...], jnp.concatenate([hot, hot], axis=0))
            sums = [jnp.zeros((8, QW), F32) for _ in range(6)]
            for i in range(8):
                mask = sub8 + 8 * i == xrow
                for c in range(6):
                    at = (i // 2) * 96 + c * 16 + (i % 2) * 8
                    sums[c] = sums[c] + jnp.where(mask, out[at : at + 8], 0.0)
            for c in range(6):
                line = jnp.sum(sums[c], axis=0, keepdims=True)
                picked[c, 2 * t : 2 * t + 1, :] = line[:, 0:128]
                picked[c, 2 * t + 1 : 2 * t + 2, :] = line[:, 128:256]
        high_rows = pl.ds(pl.multiple_of(g * 8 + 64, 8), 8)
        for j in range(3):
            even, odd = picked[2 * j], picked[2 * j + 1]
            rep[j, rows, :] = jnp.where(lane8 < 64, even, pltpu.roll(odd, 64, 1))
            rep[j, high_rows, :] = jnp.where(lane8 < 64, pltpu.roll(even, 64, 1), odd)

        def reply(half, c):
            pltpu.make_async_remote_copy(
                row(rep, g * 8 + c + 64 * half), row(got, me), sent.at[1], reply_r,
                device_id=(2 * g + half, c), device_id_type=MESH,
            ).start()

        @pl.when(g != mine)
        def _():
            for half in range(2):
                for c in range(NC):
                    reply(half, c)

        @pl.when(g == mine)
        def _():
            for half in range(2):
                for c in range(NC):

                    @pl.when((2 * g + half != span) | (c != chord))
                    def _():
                        reply(half, c)

        return carry

    lax.fori_loop(0, 8, pick, 0)
    got[:, pl.ds(me, 1), :] = rep[:, pl.ds(slot_row, 1), :]

    for h in halos:
        h.wait_recv()

    @pl.when(span == 0)
    def _():
        xbuf[:, 0:3] = jnp.zeros((4, 3, CY, NZ), F32)
        dbuf[:, 7:8, :] = jnp.zeros((3, 1, 128), F32)

    @pl.when(span == NS - 1)
    def _():
        xbuf[:, CX + 3 : CX + 6] = jnp.zeros((4, 3, CY, NZ), F32)
        dbuf[:, 136:137, :] = jnp.zeros((3, 1, 128), F32)

    @pl.when(chord == 0)
    def _():
        ybuf[:, :, 5:8, :] = jnp.zeros((2, CX, 3, NZ), F32)
        collow[...] = jnp.zeros((8, 128), F32)

    @pl.when(chord == NC - 1)
    def _():
        ybuf[:, :, CY + 8 : CY + 11, :] = jnp.zeros((2, CX, 3, NZ), F32)
        colhigh[...] = jnp.zeros((8, 128), F32)

    def plane(x, carry):
        def dx(f):
            return diff(*[xbuf[f, x + 3 + o] for o in (3, 2, 1, -1, -2, -3)])

        def dy(f):
            return diff(*[ybuf[f, x, 8 + o : 8 + CY + o, :] for o in (3, 2, 1, -1, -2, -3)])

        zrows = pl.ds(pl.multiple_of(x * CY, CY), CY)
        dp, du = dx(0), dx(1)
        fo[0, x] = xbuf[0, x + 3] - SCALE * (0.5 * dp + du + dy(1) + zb[1, zrows, :])
        fo[1, x] = xbuf[1, x + 3] - SCALE * (0.5 * du + dp)
        fo[2, x] = xbuf[2, x + 3] - SCALE * (0.5 * dx(2) + dy(0))
        fo[3, x] = xbuf[3, x + 3] - SCALE * (0.5 * dx(3) + zb[0, zrows, :])
        return carry

    lax.fori_loop(0, CX, plane, 0)
    for b in range(8):
        turned = fo[0, 4 * b : 4 * b + 4].reshape(128, NZ).T
        p0[0:1, b * 128 : (b + 1) * 128] = turned[0:1, :]

    def columns(g, carry):
        rows = pl.ds(pl.multiple_of(g * 8, 8), 8)
        xs = px[rows, :]
        for t in range(8):
            hot = jnp.where(sub_s[:, 0:128] == xs[t : t + 1], 1.0, 0.0).astype(BF16)
            ohx[:, pl.ds(pl.multiple_of((g * 8 + t) * 128, 128), 128)] = hot
        return carry

    lax.fori_loop(0, 8, columns, 0)

    some(rep, got, ND - 1, sent.at[1], reply_r).wait_recv()
    for j in range(3):
        high, low = split(got[j].T)
        lookup[j * 128 : (j + 1) * 128, 0:128] = high
        lookup[j * 128 : (j + 1) * 128, 128:256] = low

    def interp(q, carry):
        cols = pl.ds(pl.multiple_of(q * QW, QW), QW)
        totals = [jnp.zeros((8, QW), F32) for _ in range(6)]
        for k in range(K):
            hot = onehot[:, pl.ds(pl.multiple_of(k * PTS + q * QW, QW), QW)]
            out = dot(lookup[...], jnp.concatenate([hot, hot], axis=0))
            at = sub_s == rank[k : k + 1, cols]
            weight = w_ref[k : k + 1, cols]
            for c in range(6):
                part = jnp.where(at, out[c * CAP : (c + 1) * CAP], 0.0)
                totals[c] = totals[c] + weight * jnp.sum(part.reshape(8, 8, QW), axis=0)
        for c in range(6):
            motion_ref[c : c + 1, cols] = jnp.sum(totals[c], axis=0, keepdims=True)
        return carry

    lax.fori_loop(0, PTS // QW, interp, 0)

    pressure = p0[0:1, :] + (SCALE * 74.0) * motion_ref[5:6, :]
    for q in range(PTS // QW):
        cols = slice(q * QW, (q + 1) * QW)
        for k in range(K):
            ent = slice(k * PTS + q * QW, k * PTS + (q + 1) * QW)
            at = sub_s == rank[k : k + 1, cols]
            for c in range(3):
                value = nrm_ref[c : c + 1, cols] * pressure[:, cols] * w_ref[k : k + 1, cols]
                high = value.astype(BF16).astype(F32)
                loadb[c * CAP : (c + 1) * CAP, ent] = jnp.where(at, high, 0.0).astype(BF16)
                loadb[256 + c * CAP : 256 + (c + 1) * CAP, ent] = jnp.where(at, value - high, 0.0).astype(BF16)
    both = dot_nt(onehot[...], loadb[...])
    outg[0] = both[:, 0:128] + both[:, 256:384]
    outg[1] = both[:, 128:256] + both[:, 384:512]
    exchange(outg, arrived, 2, load_r)

    zlane = iota((128, NZ), 1)
    reach = jnp.where(zlane == 0, 74.0 * SCALE, jnp.where(zlane == 1, -16.0 * SCALE, jnp.where(zlane == 2, 2.0 * SCALE, 0.0)))
    for b in range(8):
        turned = jnp.broadcast_to(motion_ref[5:6, b * 128 : (b + 1) * 128], (8, 128)).T
        fix = (turned[:, 0:1] * reach).reshape(4, CY, NZ)
        fo[0, 4 * b : 4 * b + 4] = fo[0, 4 * b : 4 * b + 4] + fix

    def collect(k, carry):
        g = near_first(k)
        await_group(outg, arrived, 2, load_r, g)
        cols = pl.ds(pl.multiple_of(g * 1024, 1024), 1024)
        values = halves(arrived, 0, g) + halves(arrived, 1, g)[0:1]
        for c in range(3):
            high = values[c].astype(BF16).astype(F32)
            for half, value in enumerate((high, values[c] - high)):
                for t in range(8):
                    wide = jnp.broadcast_to(value[t : t + 1], (16, 128)).astype(BF16)
                    wide = jnp.concatenate([wide] * 4, axis=0)
                    hot = ohx[:, pl.ds(pl.multiple_of((g * 8 + t) * 128, 128), 128)]
                    at = (half * 3 + c) * 64
                    fb[at : at + 64, t * 128 : (t + 1) * 128] = hot * wide
        force[...] += dot_nt(fb[...], ohy[:, cols])
        return carry

    lax.fori_loop(0, 8, collect, 0)
    for c in range(3):
        total = force[c * 64 : (c + 1) * 64, :] + force[192 + c * 64 : 192 + (c + 1) * 64, :]
        spread[c, pl.ds(0, 64, stride=2), :] = total[:, 0:128]
        spread[c, pl.ds(1, 64, stride=2), :] = total[:, 128:256]

    lane128 = iota((128, 128), 1)
    low_t, high_t = collow[...].T, colhigh[...].T
    for c in range(3):
        mid = dbuf[c, 8:136, :]
        west = jnp.where(lane128 == 0, low_t[:, c : c + 1], pltpu.roll(mid, 1, 1))
        east = jnp.where(lane128 == 127, high_t[:, c : c + 1], pltpu.roll(mid, 127, 1))
        lap = dbuf[c, 9:137, :] + dbuf[c, 7:135, :] + east + west - 4.0 * mid
        vel = vbuf[c]
        vel_new = vel + 0.3 * (0.5 * lap + spread[c] - 0.2 * vel)
        vel_out[c] = vel_new
        disp_out[c] = mid + 0.3 * vel_new

    for h in halos:
        h.wait_send()
    for index, (src, dst) in enumerate(((req, asked), (rep, got), (outg, arrived))):
        some(src, dst, ND - 1, sent.at[index], reply_r).wait_send()


def put(fo, motion, disp, vel, fo_out, motion_out, disp_out, vel_out, sems):
    pairs = [(fo.at[i], fo_out.at[i]) for i in range(4)] + [(motion, motion_out), (disp, disp_out), (vel, vel_out)]
    copies = [pltpu.make_async_copy(a, b, sems.at[i]) for i, (a, b) in enumerate(pairs)]
    for c in copies:
        c.start()
    for c in copies:
        c.wait()


def body(fluid, disp, vel, owners, nodes, weights, normals):
    small = pl.BlockSpec(memory_space=pltpu.VMEM)
    big = pl.BlockSpec(memory_space=pltpu.HBM)
    vm = pltpu.VMEM
    dma = pltpu.SemaphoreType.DMA
    scratch = [
        vm((4, CX + 6, CY, NZ), F32),
        vm((2, CX, CY + 16, NZ), F32),
        vm((2, PTS, NZ), F32),
        vm((3, 144, 128), F32),
        vm((3, 128, 128), F32),
        vm((ND, ENT), BF16),
        vm((K, PTS), I32),
        vm((128, ENT), BF16),
        vm((1, ND, 128), F32),
        vm((1, ND, 128), F32),
        vm((CAP, 128), I32),
        vm((384, 512), BF16),
        vm((256, SLOTS), BF16),
        vm((64, SLOTS), BF16),
        vm((6, 8, 128), F32),
        vm((3, ND, 128), F32),
        vm((3, ND, 128), F32),
        vm((384, 256), BF16),
        vm((8, PTS), F32),
        vm((512, ENT), BF16),
        vm((2, ND, 128), F32),
        vm((2, ND, 128), F32),
        vm((384, 1024), BF16),
        vm((384, 256), F32),
        vm((3, 128, 128), F32),
        vm((2, 8, 128), F32),
        vm((8, 128), F32),
        vm((8, 128), F32),
        dma((5,)),
        dma((8,)),
        dma((8,)),
        dma((3,)),
        dma((8,)),
        dma(()),
        dma((8,)),
    ]
    shapes = (fluid.shape, (6, PTS), disp.shape, vel.shape)
    done = pl.pallas_call(
        kernel,
        name="coupling",
        out_shape=tuple(vm(shape, F32) for shape in shapes),
        in_specs=[small] * 4 + [big] * 3,
        out_specs=(small,) * 4,
        scratch_shapes=scratch,
        compiler_params=pltpu.CompilerParams(
            collective_id=0, has_side_effects=True, vmem_limit_bytes=64_400_000
        ),
    )(owners.T, nodes.T, weights.T, normals, fluid, disp, vel)
    return pl.pallas_call(
        put,
        name="put",
        out_shape=tuple(jax.ShapeDtypeStruct(shape, F32) for shape in shapes),
        in_specs=[small] * 4,
        out_specs=(big,) * 4,
        scratch_shapes=[dma((7,))],
        compiler_params=pltpu.CompilerParams(vmem_limit_bytes=1024 * 1024),
    )(*[pltpu.with_memory_space_constraint(part, pltpu.VMEM) for part in done])


def solution(mesh):
    block, line = P(None, "span", "chord"), P(("span", "chord"), None)
    return jax.shard_map(
        body,
        mesh=mesh,
        in_specs=(P(None, "span", "chord", None), block, block, line, line, line, P(None, ("span", "chord"))),
        out_specs=(P(None, "span", "chord", None), P(None, ("span", "chord")), block, block),
        check_vma=False,
    )
```

```python
import jax
import jax.numpy as jnp
from jax import lax
from jax.experimental import pallas as pl
from jax.experimental.pallas import tpu as pltpu
from jax.sharding import PartitionSpec as P

MESH = pl.DeviceIdType.MESH
F32, BF16, I32 = jnp.float32, jnp.bfloat16, jnp.int32
NS, NC, ND = 16, 8, 128
CAP = 64
CX, CY, NZ = 32, 32, 128
PTS, K = 1024, 4
ENT = PTS * K
SLOTS = ND * CAP
QW = 256
SCALE = 0.4 / 60.0
NT = (((1,), (1,)), ((), ()))


def iota(shape, dim):
    return lax.broadcasted_iota(I32, shape, dim)


def split(value):
    high = value.astype(BF16)
    return high, (value - high.astype(F32)).astype(BF16)


def dot(a, b):
    return jnp.dot(a, b, preferred_element_type=F32)


def dot_nt(a, b):
    return lax.dot_general(a, b, NT, preferred_element_type=F32)


def diff(far_up, mid_up, up, down, mid_down, far_down):
    return 45.0 * (up - down) - 9.0 * (mid_up - mid_down) + (far_up - far_down)


def stencil(distance):
    size = jnp.abs(distance)
    value = jnp.where(size == 1, 45.0, jnp.where(size == 2, -9.0, jnp.where(size == 3, 1.0, 0.0)))
    return jnp.where(distance > 0, value, -value)


def kernel(
    own_ref, node_ref, w_ref, nrm_ref, fluid_hbm, disp_hbm, vel_hbm,
    fo, motion_ref, disp_ref, base_ref, force,
    xbuf, ybuf, zb, dbuf, vbuf,
    onehot, rank, rankhot, reqb, req, asked, px,
    table, ohy, ohx, picked, rep, got, lookup, p0,
    loadb, outg, arrived, fb, colsend, collow, colhigh,
    in_sem, halo_s, halo_r, sent, ask_r, reply_r, load_r,
):
    span, chord = lax.axis_index("span"), lax.axis_index("chord")
    me = span * NC + chord

    mine = span // 2
    slot_row = mine * 8 + chord + 64 * lax.rem(span, 2)

    loads = [
        pltpu.make_async_copy(disp_hbm, dbuf.at[:, pl.ds(8, 128)], in_sem.at[0]),
        pltpu.make_async_copy(vel_hbm, vbuf, in_sem.at[1]),
        pltpu.make_async_copy(fluid_hbm, xbuf.at[:, pl.ds(3, CX)], in_sem.at[2]),
        pltpu.make_async_copy(fluid_hbm.at[0], ybuf.at[0, :, pl.ds(8, CY)], in_sem.at[3]),
        pltpu.make_async_copy(fluid_hbm.at[2], ybuf.at[1, :, pl.ds(8, CY)], in_sem.at[4]),
    ]
    for c in loads:
        c.start()

    barrier = pltpu.get_barrier_semaphore()

    def far_first(k):
        half = (k + 1) // 2
        return lax.rem(span + 10 + jnp.where(lax.rem(k, 2) == 1, half, 16 - half), NS)

    def each_peer(act):
        def one(k, carry):
            s = far_first(k)

            @pl.when(s != span)
            def _():
                for c in range(NC):
                    act(s, c)

            return carry

        lax.fori_loop(0, NS, one, 0)
        for c in range(NC):

            @pl.when(c != chord)
            def _():
                act(span, c)

    each_peer(lambda s, c: pl.semaphore_signal(barrier, 1, device_id=(s, c), device_id_type=MESH))

    before = (iota((QW, QW), 0) < iota((QW, QW), 1)).astype(F32).astype(BF16)
    ones = jnp.ones((QW, QW), BF16)
    sub_o = iota((ND, QW), 0)
    sub_s = iota((CAP, QW), 0)
    offset = jnp.zeros((ND, QW), F32)
    for q in range(PTS // QW):
        cols = slice(q * QW, (q + 1) * QW)
        masks = []
        count = jnp.zeros((ND, QW), F32)
        for k in range(K):
            mask = sub_o == own_ref[k : k + 1, cols]
            masks.append(mask)
            hot = jnp.where(mask, 1.0, 0.0)
            onehot[:, k * PTS + q * QW : k * PTS + (q + 1) * QW] = hot.astype(BF16)
            count = count + hot
        count = count.astype(BF16)
        prior = dot(count, before) + offset
        offset = offset + dot(count, ones)
        for k in range(K):
            slot = jnp.sum(jnp.where(masks[k], prior, 0.0), axis=0, keepdims=True).astype(I32)
            node = node_ref[k : k + 1, cols]
            ent = slice(k * PTS + q * QW, k * PTS + (q + 1) * QW)
            at = sub_s == slot
            rankhot[:, ent] = jnp.where(at, 1.0, 0.0).astype(BF16)
            reqb[0:CAP, ent] = jnp.where(at, (node // 256).astype(F32), 0.0).astype(BF16)
            reqb[CAP:, ent] = jnp.where(at, lax.rem(node, 256).astype(F32), 0.0).astype(BF16)
            rank[k : k + 1, cols] = slot
    req[0] = dot_nt(onehot[...], reqb[...])

    for c in loads:
        c.wait()
    for c in range(6):
        for odd in range(2):
            value = dbuf[c, pl.ds(8 + odd, 64, stride=2), :] if c < 3 else vbuf[c - 3, pl.ds(odd, 64, stride=2), :]
            high, low = split(value)
            for t in range(4):
                rows = slice(t * 96 + c * 16, t * 96 + (c + 1) * 16)
                table[rows, odd * 128 : (odd + 1) * 128] = high[t * 16 : (t + 1) * 16]
                table[rows, 256 + odd * 128 : 256 + (odd + 1) * 128] = low[t * 16 : (t + 1) * 16]
    for c in range(3):
        turned = dbuf[c, 8:136, :].T
        colsend[0, c : c + 1, :] = turned[0:1, :]
        colsend[1, c : c + 1, :] = turned[127:128, :]
    force[...] = jnp.zeros((384, 256), F32)

    src, tgt = iota((NZ, NZ), 0), iota((NZ, NZ), 1)
    inner = stencil(src - tgt)
    ghost = jnp.where(src < 3, stencil(-(src + 1 + tgt)), 0.0)
    for i, (f, tab) in enumerate(((0, inner + ghost), (3, inner - ghost))):
        tab = tab.astype(BF16)
        tab = jnp.concatenate([tab, tab], axis=0)
        for b in range(4):
            high, low = split(xbuf[f, 3 + 8 * b : 11 + 8 * b].reshape(256, NZ))
            zb[i, b * 256 : (b + 1) * 256, :] = dot(jnp.concatenate([high, low], axis=1), tab)

    pl.semaphore_wait(barrier, ND - 1)

    def row(ref, at):
        return ref.at[:, pl.ds(at, 1)]

    def exchange(src, dst, index, recv):
        def send(s, c):
            pltpu.make_async_remote_copy(
                row(src, s * NC + c), row(dst, slot_row), sent.at[index], recv.at[mine],
                device_id=(s, c), device_id_type=MESH,
            ).start()

        each_peer(send)
        dst[:, pl.ds(slot_row, 1), :] = src[:, pl.ds(me, 1), :]

    def some(src, dst, count, send_sem, recv_sem):
        return pltpu.make_async_remote_copy(
            src.at[:, pl.ds(0, count)], dst.at[:, pl.ds(0, count)], send_sem, recv_sem,
            device_id=(span, chord), device_id_type=MESH,
        )

    def await_group(src, dst, index, recv, g):
        @pl.when(g == mine)
        def _():
            some(src, dst, 15, sent.at[index], recv.at[g]).wait_recv()

        @pl.when(g != mine)
        def _():
            some(src, dst, 16, sent.at[index], recv.at[g]).wait_recv()

    def near_first(k):
        half = (k + 1) // 2
        return lax.rem(mine + jnp.where(lax.rem(k, 2) == 1, half, 8 - half), 8)

    def round_trip(k):
        step = jnp.where(k < 2, k, jnp.where(k < 4, k + 2, jnp.where(k == 4, 3, jnp.where(k == 5, 6, 2))))
        return lax.rem(mine + jnp.where(k == 7, 7, step), 8)

    exchange(req, asked, 0, ask_r)

    up = (lax.rem(span + 1, NS), chord)
    down = (lax.rem(span + NS - 1, NS), chord)
    right = (span, lax.rem(chord + 1, NC))
    left = (span, lax.rem(chord + NC - 1, NC))
    moves = [
        (xbuf.at[:, pl.ds(CX, 3)], xbuf.at[:, pl.ds(0, 3)], up),
        (xbuf.at[:, pl.ds(3, 3)], xbuf.at[:, pl.ds(CX + 3, 3)], down),
        (ybuf.at[:, :, pl.ds(CY + 5, 3)], ybuf.at[:, :, pl.ds(5, 3)], right),
        (ybuf.at[:, :, pl.ds(8, 3)], ybuf.at[:, :, pl.ds(CY + 8, 3)], left),
        (dbuf.at[:, pl.ds(135, 1)], dbuf.at[:, pl.ds(7, 1)], up),
        (dbuf.at[:, pl.ds(8, 1)], dbuf.at[:, pl.ds(136, 1)], down),
        (colsend.at[1], collow, right),
        (colsend.at[0], colhigh, left),
    ]
    halos = [
        pltpu.make_async_remote_copy(a, b, halo_s.at[i], halo_r.at[i], device_id=to, device_id_type=MESH)
        for i, (a, b, to) in enumerate(moves)
    ]
    for h in halos:
        h.start()

    lane8 = iota((8, 128), 1)
    sub8f = iota((8, QW), 0).astype(F32)
    low_y = iota((256, QW), 0).astype(F32).astype(BF16)
    low_x = iota((64, 128), 0).astype(F32).astype(BF16)
    one, zero = jnp.ones((), BF16), jnp.zeros((), BF16)

    def tall(line, rows):
        wide = jnp.broadcast_to(line, (16, line.shape[1])).astype(BF16)
        return jnp.concatenate([wide] * (rows // 16), axis=0)

    def hot_rows(numbers, line, rows):
        return jnp.where(numbers == tall(line, rows), one, zero)

    def halves(ref, j, g):
        low = ref[j, pl.ds(pl.multiple_of(g * 8, 8), 8), :]
        high = ref[j, pl.ds(pl.multiple_of(g * 8 + 64, 8), 8), :]
        front = jnp.where(lane8 < 64, low, pltpu.roll(high, 64, 1))
        back = jnp.where(lane8 < 64, pltpu.roll(low, 64, 1), high)
        return front, back

    def pick(k, carry):
        g = round_trip(k)
        await_group(req, asked, 0, ask_r, g)
        rows = pl.ds(pl.multiple_of(g * 8, 8), 8)
        xs, ys = halves(asked, 0, g)
        px[rows, :] = xs
        group = [pl.ds(pl.multiple_of((g * 4 + t) * QW, QW), QW) for t in range(4)]
        for t in range(4):
            yrow = jnp.concatenate([ys[2 * t : 2 * t + 1], ys[2 * t + 1 : 2 * t + 2]], axis=1)
            ohy[:, group[t]] = hot_rows(low_y, yrow, 256)
        for t in range(4):
            xrow = jnp.concatenate([xs[2 * t : 2 * t + 1], xs[2 * t + 1 : 2 * t + 2]], axis=1)
            hot = ohy[:, group[t]]
            out = dot(table[...], jnp.concatenate([hot, hot], axis=0))
            sums = [jnp.zeros((8, QW), F32) for _ in range(6)]
            for i in range(8):
                mask = sub8f + 8.0 * i == xrow
                for c in range(6):
                    at = (i // 2) * 96 + c * 16 + (i % 2) * 8
                    sums[c] = sums[c] + jnp.where(mask, out[at : at + 8], 0.0)
            for c in range(6):
                line = jnp.sum(sums[c], axis=0, keepdims=True)
                picked[c, 2 * t : 2 * t + 1, :] = line[:, 0:128]
                picked[c, 2 * t + 1 : 2 * t + 2, :] = line[:, 128:256]
        high_rows = pl.ds(pl.multiple_of(g * 8 + 64, 8), 8)
        for j in range(3):
            even, odd = picked[2 * j], picked[2 * j + 1]
            rep[j, rows, :] = jnp.where(lane8 < 64, even, pltpu.roll(odd, 64, 1))
            rep[j, high_rows, :] = jnp.where(lane8 < 64, pltpu.roll(even, 64, 1), odd)

        def reply(half, c):
            pltpu.make_async_remote_copy(
                row(rep, g * 8 + c + 64 * half), row(got, me), sent.at[1], reply_r,
                device_id=(2 * g + half, c), device_id_type=MESH,
            ).start()

        @pl.when(g != mine)
        def _():
            for half in range(2):
                for c in range(NC):
                    reply(half, c)

        @pl.when(g == mine)
        def _():
            for half in range(2):
                for c in range(NC):

                    @pl.when((2 * g + half != span) | (c != chord))
                    def _():
                        reply(half, c)

        return carry

    lax.fori_loop(0, 8, pick, 0)
    got[:, pl.ds(me, 1), :] = rep[:, pl.ds(slot_row, 1), :]

    for h in halos:
        h.wait_recv()

    @pl.when(span == 0)
    def _():
        xbuf[:, 0:3] = jnp.zeros((4, 3, CY, NZ), F32)
        dbuf[:, 7:8, :] = jnp.zeros((3, 1, 128), F32)

    @pl.when(span == NS - 1)
    def _():
        xbuf[:, CX + 3 : CX + 6] = jnp.zeros((4, 3, CY, NZ), F32)
        dbuf[:, 136:137, :] = jnp.zeros((3, 1, 128), F32)

    @pl.when(chord == 0)
    def _():
        ybuf[:, :, 5:8, :] = jnp.zeros((2, CX, 3, NZ), F32)
        collow[...] = jnp.zeros((8, 128), F32)

    @pl.when(chord == NC - 1)
    def _():
        ybuf[:, :, CY + 8 : CY + 11, :] = jnp.zeros((2, CX, 3, NZ), F32)
        colhigh[...] = jnp.zeros((8, 128), F32)

    def plane(x, carry):
        def dx(f):
            return diff(*[xbuf[f, x + 3 + o] for o in (3, 2, 1, -1, -2, -3)])

        def dy(f):
            return diff(*[ybuf[f, x, 8 + o : 8 + CY + o, :] for o in (3, 2, 1, -1, -2, -3)])

        zrows = pl.ds(pl.multiple_of(x * CY, CY), CY)
        dp, du = dx(0), dx(1)
        fo[0, x] = xbuf[0, x + 3] - SCALE * (0.5 * dp + du + dy(1) + zb[1, zrows, :])
        fo[1, x] = xbuf[1, x + 3] - SCALE * (0.5 * du + dp)
        fo[2, x] = xbuf[2, x + 3] - SCALE * (0.5 * dx(2) + dy(0))
        fo[3, x] = xbuf[3, x + 3] - SCALE * (0.5 * dx(3) + zb[0, zrows, :])
        return carry

    lax.fori_loop(0, CX, plane, 0)
    for b in range(8):
        turned = fo[0, 4 * b : 4 * b + 4].reshape(128, NZ).T
        p0[0:1, b * 128 : (b + 1) * 128] = turned[0:1, :]

    def columns(g, carry):
        rows = pl.ds(pl.multiple_of(g * 8, 8), 8)
        xs = px[rows, :]
        for t in range(8):
            ohx[:, pl.ds(pl.multiple_of((g * 8 + t) * 128, 128), 128)] = hot_rows(low_x, xs[t : t + 1], 64)
        return carry

    lax.fori_loop(0, 8, columns, 0)

    some(rep, got, ND - 1, sent.at[1], reply_r).wait_recv()
    for j in range(3):
        high, low = split(got[j].T)
        for c in range(2):
            for t in range(4):
                at = t * 96 + (2 * j + c) * 16
                lookup[at : at + 16, 0:128] = high[c * 64 + t * 16 : c * 64 + (t + 1) * 16]
                lookup[at : at + 16, 128:256] = low[c * 64 + t * 16 : c * 64 + (t + 1) * 16]

    sub8i = iota((8, QW), 0)

    def interp(q, carry):
        cols = pl.ds(pl.multiple_of(q * QW, QW), QW)
        totals = [jnp.zeros((8, QW), F32) for _ in range(6)]
        for k in range(K):
            hot = onehot[:, pl.ds(pl.multiple_of(k * PTS + q * QW, QW), QW)]
            out = dot(lookup[...], jnp.concatenate([hot, hot], axis=0))
            slot = rank[k : k + 1, cols]
            weight = w_ref[k : k + 1, cols]
            sums = [jnp.zeros((8, QW), F32) for _ in range(6)]
            for i in range(8):
                mask = sub8i + 8 * i == slot
                for c in range(6):
                    at = (i // 2) * 96 + c * 16 + (i % 2) * 8
                    sums[c] = sums[c] + jnp.where(mask, out[at : at + 8], 0.0)
            for c in range(6):
                totals[c] = totals[c] + weight * sums[c]
        for c in range(6):
            motion_ref[c : c + 1, cols] = jnp.sum(totals[c], axis=0, keepdims=True)
        return carry

    lax.fori_loop(0, PTS // QW, interp, 0)

    pressure = p0[0:1, :] + (SCALE * 74.0) * motion_ref[5:6, :]
    both = jnp.zeros((ND, 384), F32)
    push = [nrm_ref[c : c + 1, :] * pressure for c in range(3)]
    for k in range(K):
        ent = slice(k * PTS, (k + 1) * PTS)
        for c in range(3):
            value = push[c] * w_ref[k : k + 1, :]
            high = value.astype(BF16).astype(F32)
            for half, part in enumerate((high, value - high)):
                at = (c + 2 * half) * CAP if c < 2 else (4 + half) * CAP
                loadb[at : at + CAP, ent] = rankhot[:, ent] * tall(part, CAP)
        both = both + dot_nt(onehot[:, ent], loadb[:, ent])
    outg[0] = both[:, 0:128] + both[:, 128:256]
    outg[1] = both[:, 256:384] + pltpu.roll(both[:, 256:384], 64, 1)
    exchange(outg, arrived, 2, load_r)

    zlane = iota((128, NZ), 1)
    reach = jnp.where(zlane == 0, 74.0 * SCALE, jnp.where(zlane == 1, -16.0 * SCALE, jnp.where(zlane == 2, 2.0 * SCALE, 0.0)))
    for b in range(8):
        turned = jnp.broadcast_to(motion_ref[5:6, b * 128 : (b + 1) * 128], (8, 128)).T
        fix = (turned[:, 0:1] * reach).reshape(4, CY, NZ)
        fo[0, 4 * b : 4 * b + 4] = fo[0, 4 * b : 4 * b + 4] + fix

    lane128 = iota((128, 128), 1)
    low_t, high_t = collow[...].T, colhigh[...].T
    for c in range(3):
        mid = dbuf[c, 8:136, :]
        west = jnp.where(lane128 == 0, low_t[:, c : c + 1], pltpu.roll(mid, 1, 1))
        east = jnp.where(lane128 == 127, high_t[:, c : c + 1], pltpu.roll(mid, 127, 1))
        lap = dbuf[c, 9:137, :] + dbuf[c, 7:135, :] + east + west - 4.0 * mid
        vel = vbuf[c]
        base_ref[c] = vel + 0.3 * (0.5 * lap - 0.2 * vel)
        disp_ref[c] = mid

    def collect(k, carry):
        g = near_first(k)
        await_group(outg, arrived, 2, load_r, g)
        cols = pl.ds(pl.multiple_of(g * 1024, 1024), 1024)
        values = halves(arrived, 0, g) + halves(arrived, 1, g)[0:1]
        for c in range(3):
            high = values[c].astype(BF16).astype(F32)
            for half, value in enumerate((high, values[c] - high)):
                for t in range(8):
                    hot = ohx[:, pl.ds(pl.multiple_of((g * 8 + t) * 128, 128), 128)]
                    at = (half * 3 + c) * 64
                    fb[at : at + 64, t * 128 : (t + 1) * 128] = hot * tall(value[t : t + 1], 64)
        force[...] += dot_nt(fb[...], ohy[:, cols])
        return carry

    lax.fori_loop(0, 8, collect, 0)
    for h in halos:
        h.wait_send()
    for index, (src, dst) in enumerate(((req, asked), (rep, got), (outg, arrived))):
        some(src, dst, ND - 1, sent.at[index], reply_r).wait_send()


def finish(fo, motion, disp, base, force, fo_out, motion_out, disp_out, vel_out, disp_new, vel_new, sems):
    pairs = [(fo.at[i], fo_out.at[i]) for i in range(4)] + [(motion, motion_out), (disp_new, disp_out), (vel_new, vel_out)]
    copies = [pltpu.make_async_copy(a, b, sems.at[i]) for i, (a, b) in enumerate(pairs)]
    for c in copies[:5]:
        c.start()
    for c in range(3):
        total = force[c * 64 : (c + 1) * 64, :] + force[192 + c * 64 : 192 + (c + 1) * 64, :]
        for odd in range(2):
            rows = pl.ds(odd, 64, stride=2)
            vel = base[c, rows, :] + 0.3 * total[:, odd * 128 : (odd + 1) * 128]
            vel_new[c, rows, :] = vel
            disp_new[c, rows, :] = disp[c, rows, :] + 0.3 * vel
    for c in copies[5:]:
        c.start()
    for c in copies:
        c.wait()


def body(fluid, disp, vel, owners, nodes, weights, normals):
    small = pl.BlockSpec(memory_space=pltpu.VMEM)
    big = pl.BlockSpec(memory_space=pltpu.HBM)
    vm = pltpu.VMEM
    dma = pltpu.SemaphoreType.DMA
    scratch = [
        vm((4, CX + 6, CY, NZ), F32),
        vm((2, CX, CY + 16, NZ), F32),
        vm((2, PTS, NZ), F32),
        vm((3, 144, 128), F32),
        vm((3, 128, 128), F32),
        vm((ND, ENT), BF16),
        vm((K, PTS), I32),
        vm((CAP, ENT), BF16),
        vm((128, ENT), BF16),
        vm((1, ND, 128), F32),
        vm((1, ND, 128), F32),
        vm((CAP, 128), F32),
        vm((384, 512), BF16),
        vm((256, SLOTS), BF16),
        vm((64, SLOTS), BF16),
        vm((6, 8, 128), F32),
        vm((3, ND, 128), F32),
        vm((3, ND, 128), F32),
        vm((384, 256), BF16),
        vm((8, PTS), F32),
        vm((384, ENT), BF16),
        vm((2, ND, 128), F32),
        vm((2, ND, 128), F32),
        vm((384, 1024), BF16),
        vm((2, 8, 128), F32),
        vm((8, 128), F32),
        vm((8, 128), F32),
        dma((5,)),
        dma((8,)),
        dma((8,)),
        dma((3,)),
        dma((8,)),
        dma(()),
        dma((8,)),
    ]
    shapes = (fluid.shape, (6, PTS), disp.shape, vel.shape)
    kept = shapes + ((384, 256),)
    done = pl.pallas_call(
        kernel,
        name="coupling",
        out_shape=tuple(vm(shape, F32) for shape in kept),
        in_specs=[small] * 4 + [big] * 3,
        out_specs=(small,) * 5,
        scratch_shapes=scratch,
        compiler_params=pltpu.CompilerParams(
            collective_id=0, has_side_effects=True, vmem_limit_bytes=64_000_000
        ),
    )(owners.T, nodes.T, weights.T, normals, fluid, disp, vel)
    return pl.pallas_call(
        finish,
        name="finish",
        out_shape=tuple(jax.ShapeDtypeStruct(shape, F32) for shape in shapes),
        in_specs=[small] * 5,
        out_specs=(big,) * 4,
        scratch_shapes=[vm(disp.shape, F32), vm(vel.shape, F32), dma((7,))],
        compiler_params=pltpu.CompilerParams(vmem_limit_bytes=1024 * 1024),
    )(*[pltpu.with_memory_space_constraint(part, pltpu.VMEM) for part in done])


def solution(mesh):
    block, line = P(None, "span", "chord"), P(("span", "chord"), None)
    return jax.shard_map(
        body,
        mesh=mesh,
        in_specs=(P(None, "span", "chord", None), block, block, line, line, line, P(None, ("span", "chord"))),
        out_specs=(P(None, "span", "chord", None), P(None, ("span", "chord")), block, block),
        check_vma=False,
    )
```

```python
import jax
import jax.numpy as jnp
from jax import lax
from jax.experimental import pallas as pl
from jax.experimental.pallas import tpu as pltpu
from jax.sharding import PartitionSpec as P

MESH = pl.DeviceIdType.MESH
F32, BF16, I32 = jnp.float32, jnp.bfloat16, jnp.int32
NS, NC, ND = 16, 8, 128
CAP = 64
CX, CY, NZ = 32, 32, 128
PTS, K = 1024, 4
ENT = PTS * K
SLOTS = ND * CAP
QW = 256
SCALE = 0.4 / 60.0
NT = (((1,), (1,)), ((), ()))


def iota(shape, dim):
    return lax.broadcasted_iota(I32, shape, dim)


def split(value):
    high = value.astype(BF16)
    return high, (value - high.astype(F32)).astype(BF16)


def dot(a, b):
    return jnp.dot(a, b, preferred_element_type=F32)


def dot_nt(a, b):
    return lax.dot_general(a, b, NT, preferred_element_type=F32)


def diff(far_up, mid_up, up, down, mid_down, far_down):
    return 45.0 * (up - down) - 9.0 * (mid_up - mid_down) + (far_up - far_down)


def stencil(distance):
    size = jnp.abs(distance)
    value = jnp.where(size == 1, 45.0, jnp.where(size == 2, -9.0, jnp.where(size == 3, 1.0, 0.0)))
    return jnp.where(distance > 0, value, -value)


def kernel(
    own_ref, node_ref, w_ref, nrm_ref, fluid_hbm, disp_hbm, vel_hbm,
    fo, motion_ref, disp_ref, base_ref, force,
    xbuf, ybuf, zb, dbuf, vbuf,
    onehot, rank, rankhot, reqb, req, asked, px,
    table, ohy, ohx, picked, rep, got, lookup, p0,
    loadb, outg, arrived, fb, colsend, collow, colhigh,
    in_sem, halo_s, halo_r, sent, ask_r, reply_r, load_r,
):
    span, chord = lax.axis_index("span"), lax.axis_index("chord")
    me = span * NC + chord

    mine = span // 2
    slot_row = mine * 8 + chord + 64 * lax.rem(span, 2)

    loads = [
        pltpu.make_async_copy(disp_hbm, dbuf.at[:, pl.ds(8, 128)], in_sem.at[0]),
        pltpu.make_async_copy(vel_hbm, vbuf, in_sem.at[1]),
        pltpu.make_async_copy(fluid_hbm, xbuf.at[:, pl.ds(3, CX)], in_sem.at[2]),
        pltpu.make_async_copy(fluid_hbm.at[0], ybuf.at[0, :, pl.ds(8, CY)], in_sem.at[3]),
        pltpu.make_async_copy(fluid_hbm.at[2], ybuf.at[1, :, pl.ds(8, CY)], in_sem.at[4]),
    ]
    for c in loads:
        c.start()

    barrier = pltpu.get_barrier_semaphore()

    def late_first(k, across):
        a, b = k // 4, lax.rem(k, 4)
        z = jnp.where(a < 2, 2 + a, 3 - a) if across == 4 else 1 - a
        x = jnp.where(b == 0, 2, jnp.where(b == 3, 0, 2 * b - 1))
        return x * across + z

    def each_peer(act, backward=False):
        def one(k, carry):
            s = late_first(NS - 1 - k if backward else k, 4)

            @pl.when(s != span)
            def _():
                for c in range(NC):
                    act(s, c)

            return carry

        lax.fori_loop(0, NS, one, 0)
        for c in range(NC):

            @pl.when(c != chord)
            def _():
                act(span, c)

    each_peer(lambda s, c: pl.semaphore_signal(barrier, 1, device_id=(s, c), device_id_type=MESH), True)

    before = (iota((QW, QW), 0) < iota((QW, QW), 1)).astype(F32).astype(BF16)
    ones = jnp.ones((QW, QW), BF16)
    sub_o = iota((ND, QW), 0)
    sub_s = iota((CAP, QW), 0)
    offset = jnp.zeros((ND, QW), F32)
    for q in range(PTS // QW):
        cols = slice(q * QW, (q + 1) * QW)
        masks = []
        count = jnp.zeros((ND, QW), F32)
        for k in range(K):
            mask = sub_o == own_ref[k : k + 1, cols]
            masks.append(mask)
            hot = jnp.where(mask, 1.0, 0.0)
            onehot[:, k * PTS + q * QW : k * PTS + (q + 1) * QW] = hot.astype(BF16)
            count = count + hot
        count = count.astype(BF16)
        prior = dot(count, before) + offset
        offset = offset + dot(count, ones)
        for k in range(K):
            slot = jnp.sum(jnp.where(masks[k], prior, 0.0), axis=0, keepdims=True).astype(I32)
            node = node_ref[k : k + 1, cols]
            ent = slice(k * PTS + q * QW, k * PTS + (q + 1) * QW)
            at = sub_s == slot
            rankhot[:, ent] = jnp.where(at, 1.0, 0.0).astype(BF16)
            reqb[0:CAP, ent] = jnp.where(at, (node // 256).astype(F32), 0.0).astype(BF16)
            reqb[CAP:, ent] = jnp.where(at, lax.rem(node, 256).astype(F32), 0.0).astype(BF16)
            rank[k : k + 1, cols] = slot
    req[0] = dot_nt(onehot[...], reqb[...])

    for c in loads:
        c.wait()
    for c in range(6):
        for odd in range(2):
            value = dbuf[c, pl.ds(8 + odd, 64, stride=2), :] if c < 3 else vbuf[c - 3, pl.ds(odd, 64, stride=2), :]
            high, low = split(value)
            for t in range(4):
                rows = slice(t * 96 + c * 16, t * 96 + (c + 1) * 16)
                table[rows, odd * 128 : (odd + 1) * 128] = high[t * 16 : (t + 1) * 16]
                table[rows, 256 + odd * 128 : 256 + (odd + 1) * 128] = low[t * 16 : (t + 1) * 16]
    for c in range(3):
        turned = dbuf[c, 8:136, :].T
        colsend[0, c : c + 1, :] = turned[0:1, :]
        colsend[1, c : c + 1, :] = turned[127:128, :]
    force[...] = jnp.zeros((384, 256), F32)

    src, tgt = iota((NZ, NZ), 0), iota((NZ, NZ), 1)
    inner = stencil(src - tgt)
    ghost = jnp.where(src < 3, stencil(-(src + 1 + tgt)), 0.0)
    for i, (f, tab) in enumerate(((0, inner + ghost), (3, inner - ghost))):
        tab = tab.astype(BF16)
        tab = jnp.concatenate([tab, tab], axis=0)
        for b in range(4):
            high, low = split(xbuf[f, 3 + 8 * b : 11 + 8 * b].reshape(256, NZ))
            zb[i, b * 256 : (b + 1) * 256, :] = dot(jnp.concatenate([high, low], axis=1), tab)

    pl.semaphore_wait(barrier, ND - 1)

    def row(ref, at):
        return ref.at[:, pl.ds(at, 1)]

    def exchange(src, dst, index, recv):
        def send(s, c):
            pltpu.make_async_remote_copy(
                row(src, s * NC + c), row(dst, slot_row), sent.at[index], recv.at[mine],
                device_id=(s, c), device_id_type=MESH,
            ).start()

        each_peer(send)
        dst[:, pl.ds(slot_row, 1), :] = src[:, pl.ds(me, 1), :]

    def some(src, dst, count, send_sem, recv_sem):
        return pltpu.make_async_remote_copy(
            src.at[:, pl.ds(0, count)], dst.at[:, pl.ds(0, count)], send_sem, recv_sem,
            device_id=(span, chord), device_id_type=MESH,
        )

    def await_group(src, dst, index, recv, g):
        @pl.when(g == mine)
        def _():
            some(src, dst, 15, sent.at[index], recv.at[g]).wait_recv()

        @pl.when(g != mine)
        def _():
            some(src, dst, 16, sent.at[index], recv.at[g]).wait_recv()

    exchange(req, asked, 0, ask_r)

    up = (lax.rem(span + 1, NS), chord)
    down = (lax.rem(span + NS - 1, NS), chord)
    right = (span, lax.rem(chord + 1, NC))
    left = (span, lax.rem(chord + NC - 1, NC))
    moves = [
        (xbuf.at[:, pl.ds(CX, 3)], xbuf.at[:, pl.ds(0, 3)], up),
        (xbuf.at[:, pl.ds(3, 3)], xbuf.at[:, pl.ds(CX + 3, 3)], down),
        (ybuf.at[:, :, pl.ds(CY + 5, 3)], ybuf.at[:, :, pl.ds(5, 3)], right),
        (ybuf.at[:, :, pl.ds(8, 3)], ybuf.at[:, :, pl.ds(CY + 8, 3)], left),
        (dbuf.at[:, pl.ds(135, 1)], dbuf.at[:, pl.ds(7, 1)], up),
        (dbuf.at[:, pl.ds(8, 1)], dbuf.at[:, pl.ds(136, 1)], down),
        (colsend.at[1], collow, right),
        (colsend.at[0], colhigh, left),
    ]
    halos = [
        pltpu.make_async_remote_copy(a, b, halo_s.at[i], halo_r.at[i], device_id=to, device_id_type=MESH)
        for i, (a, b, to) in enumerate(moves)
    ]
    for h in halos:
        h.start()

    lane8 = iota((8, 128), 1)
    sub8f = iota((8, QW), 0).astype(F32)
    low_y = iota((256, QW), 0).astype(F32).astype(BF16)
    low_x = iota((64, 128), 0).astype(F32).astype(BF16)
    one, zero = jnp.ones((), BF16), jnp.zeros((), BF16)

    def tall(line, rows):
        wide = jnp.broadcast_to(line, (16, line.shape[1])).astype(BF16)
        return jnp.concatenate([wide] * (rows // 16), axis=0)

    def hot_rows(numbers, line, rows):
        return jnp.where(numbers == tall(line, rows), one, zero)

    def halves(ref, j, g):
        low = ref[j, pl.ds(pl.multiple_of(g * 8, 8), 8), :]
        high = ref[j, pl.ds(pl.multiple_of(g * 8 + 64, 8), 8), :]
        front = jnp.where(lane8 < 64, low, pltpu.roll(high, 64, 1))
        back = jnp.where(lane8 < 64, pltpu.roll(low, 64, 1), high)
        return front, back

    def pick(k, carry):
        g = late_first(k, 2)
        await_group(req, asked, 0, ask_r, g)
        rows = pl.ds(pl.multiple_of(g * 8, 8), 8)
        xs, ys = halves(asked, 0, g)
        px[rows, :] = xs
        group = [pl.ds(pl.multiple_of((g * 4 + t) * QW, QW), QW) for t in range(4)]
        for t in range(4):
            yrow = jnp.concatenate([ys[2 * t : 2 * t + 1], ys[2 * t + 1 : 2 * t + 2]], axis=1)
            ohy[:, group[t]] = hot_rows(low_y, yrow, 256)
        for t in range(4):
            xrow = jnp.concatenate([xs[2 * t : 2 * t + 1], xs[2 * t + 1 : 2 * t + 2]], axis=1)
            hot = ohy[:, group[t]]
            out = dot(table[...], jnp.concatenate([hot, hot], axis=0))
            sums = [jnp.zeros((8, QW), F32) for _ in range(6)]
            for i in range(8):
                mask = sub8f + 8.0 * i == xrow
                for c in range(6):
                    at = (i // 2) * 96 + c * 16 + (i % 2) * 8
                    sums[c] = sums[c] + jnp.where(mask, out[at : at + 8], 0.0)
            for c in range(6):
                line = jnp.sum(sums[c], axis=0, keepdims=True)
                picked[c, 2 * t : 2 * t + 1, :] = line[:, 0:128]
                picked[c, 2 * t + 1 : 2 * t + 2, :] = line[:, 128:256]
        high_rows = pl.ds(pl.multiple_of(g * 8 + 64, 8), 8)
        for j in range(3):
            even, odd = picked[2 * j], picked[2 * j + 1]
            rep[j, rows, :] = jnp.where(lane8 < 64, even, pltpu.roll(odd, 64, 1))
            rep[j, high_rows, :] = jnp.where(lane8 < 64, pltpu.roll(even, 64, 1), odd)

        def reply(half, c):
            pltpu.make_async_remote_copy(
                row(rep, g * 8 + c + 64 * half), row(got, me), sent.at[1], reply_r,
                device_id=(2 * g + half, c), device_id_type=MESH,
            ).start()

        @pl.when(g != mine)
        def _():
            for half in range(2):
                for c in range(NC):
                    reply(half, c)

        @pl.when(g == mine)
        def _():
            for half in range(2):
                for c in range(NC):

                    @pl.when((2 * g + half != span) | (c != chord))
                    def _():
                        reply(half, c)

        return carry

    lax.fori_loop(0, 8, pick, 0)
    got[:, pl.ds(me, 1), :] = rep[:, pl.ds(slot_row, 1), :]

    for h in halos:
        h.wait_recv()

    @pl.when(span == 0)
    def _():
        xbuf[:, 0:3] = jnp.zeros((4, 3, CY, NZ), F32)
        dbuf[:, 7:8, :] = jnp.zeros((3, 1, 128), F32)

    @pl.when(span == NS - 1)
    def _():
        xbuf[:, CX + 3 : CX + 6] = jnp.zeros((4, 3, CY, NZ), F32)
        dbuf[:, 136:137, :] = jnp.zeros((3, 1, 128), F32)

    @pl.when(chord == 0)
    def _():
        ybuf[:, :, 5:8, :] = jnp.zeros((2, CX, 3, NZ), F32)
        collow[...] = jnp.zeros((8, 128), F32)

    @pl.when(chord == NC - 1)
    def _():
        ybuf[:, :, CY + 8 : CY + 11, :] = jnp.zeros((2, CX, 3, NZ), F32)
        colhigh[...] = jnp.zeros((8, 128), F32)

    def plane(x, carry):
        def dx(f):
            return diff(*[xbuf[f, x + 3 + o] for o in (3, 2, 1, -1, -2, -3)])

        def dy(f):
            return diff(*[ybuf[f, x, 8 + o : 8 + CY + o, :] for o in (3, 2, 1, -1, -2, -3)])

        zrows = pl.ds(pl.multiple_of(x * CY, CY), CY)
        dp, du = dx(0), dx(1)
        fo[0, x] = xbuf[0, x + 3] - SCALE * (0.5 * dp + du + dy(1) + zb[1, zrows, :])
        fo[1, x] = xbuf[1, x + 3] - SCALE * (0.5 * du + dp)
        fo[2, x] = xbuf[2, x + 3] - SCALE * (0.5 * dx(2) + dy(0))
        fo[3, x] = xbuf[3, x + 3] - SCALE * (0.5 * dx(3) + zb[0, zrows, :])
        return carry

    lax.fori_loop(0, CX, plane, 0)
    for b in range(8):
        turned = fo[0, 4 * b : 4 * b + 4].reshape(128, NZ).T
        p0[0:1, b * 128 : (b + 1) * 128] = turned[0:1, :]

    def columns(g, carry):
        rows = pl.ds(pl.multiple_of(g * 8, 8), 8)
        xs = px[rows, :]
        for t in range(8):
            ohx[:, pl.ds(pl.multiple_of((g * 8 + t) * 128, 128), 128)] = hot_rows(low_x, xs[t : t + 1], 64)
        return carry

    lax.fori_loop(0, 8, columns, 0)

    some(rep, got, ND - 1, sent.at[1], reply_r).wait_recv()
    for j in range(3):
        high, low = split(got[j].T)
        for c in range(2):
            for t in range(4):
                at = t * 96 + (2 * j + c) * 16
                lookup[at : at + 16, 0:128] = high[c * 64 + t * 16 : c * 64 + (t + 1) * 16]
                lookup[at : at + 16, 128:256] = low[c * 64 + t * 16 : c * 64 + (t + 1) * 16]

    sub8i = iota((8, QW), 0)

    def interp(q, carry):
        cols = pl.ds(pl.multiple_of(q * QW, QW), QW)
        totals = [jnp.zeros((8, QW), F32) for _ in range(6)]
        for k in range(K):
            hot = onehot[:, pl.ds(pl.multiple_of(k * PTS + q * QW, QW), QW)]
            out = dot(lookup[...], jnp.concatenate([hot, hot], axis=0))
            slot = rank[k : k + 1, cols]
            weight = w_ref[k : k + 1, cols]
            sums = [jnp.zeros((8, QW), F32) for _ in range(6)]
            for i in range(8):
                mask = sub8i + 8 * i == slot
                for c in range(6):
                    at = (i // 2) * 96 + c * 16 + (i % 2) * 8
                    sums[c] = sums[c] + jnp.where(mask, out[at : at + 8], 0.0)
            for c in range(6):
                totals[c] = totals[c] + weight * sums[c]
        for c in range(6):
            motion_ref[c : c + 1, cols] = jnp.sum(totals[c], axis=0, keepdims=True)
        return carry

    lax.fori_loop(0, PTS // QW, interp, 0)

    pressure = p0[0:1, :] + (SCALE * 74.0) * motion_ref[5:6, :]
    both = jnp.zeros((ND, 384), F32)
    push = [nrm_ref[c : c + 1, :] * pressure for c in range(3)]
    for k in range(K):
        ent = slice(k * PTS, (k + 1) * PTS)
        for c in range(3):
            value = push[c] * w_ref[k : k + 1, :]
            high = value.astype(BF16).astype(F32)
            for half, part in enumerate((high, value - high)):
                at = (c + 2 * half) * CAP if c < 2 else (4 + half) * CAP
                loadb[at : at + CAP, ent] = rankhot[:, ent] * tall(part, CAP)
        both = both + dot_nt(onehot[:, ent], loadb[:, ent])
    outg[0] = both[:, 0:128] + both[:, 128:256]
    outg[1] = both[:, 256:384] + pltpu.roll(both[:, 256:384], 64, 1)
    exchange(outg, arrived, 2, load_r)

    zlane = iota((128, NZ), 1)
    reach = jnp.where(zlane == 0, 74.0 * SCALE, jnp.where(zlane == 1, -16.0 * SCALE, jnp.where(zlane == 2, 2.0 * SCALE, 0.0)))
    for b in range(8):
        turned = jnp.broadcast_to(motion_ref[5:6, b * 128 : (b + 1) * 128], (8, 128)).T
        fix = (turned[:, 0:1] * reach).reshape(4, CY, NZ)
        fo[0, 4 * b : 4 * b + 4] = fo[0, 4 * b : 4 * b + 4] + fix

    lane128 = iota((128, 128), 1)
    low_t, high_t = collow[...].T, colhigh[...].T
    for c in range(3):
        mid = dbuf[c, 8:136, :]
        west = jnp.where(lane128 == 0, low_t[:, c : c + 1], pltpu.roll(mid, 1, 1))
        east = jnp.where(lane128 == 127, high_t[:, c : c + 1], pltpu.roll(mid, 127, 1))
        lap = dbuf[c, 9:137, :] + dbuf[c, 7:135, :] + east + west - 4.0 * mid
        vel = vbuf[c]
        base_ref[c] = vel + 0.3 * (0.5 * lap - 0.2 * vel)
        disp_ref[c] = mid

    def collect(k, carry):
        g = late_first(k, 2)
        await_group(outg, arrived, 2, load_r, g)
        cols = pl.ds(pl.multiple_of(g * 1024, 1024), 1024)
        values = halves(arrived, 0, g) + halves(arrived, 1, g)[0:1]
        for c in range(3):
            high = values[c].astype(BF16).astype(F32)
            for half, value in enumerate((high, values[c] - high)):
                for t in range(8):
                    hot = ohx[:, pl.ds(pl.multiple_of((g * 8 + t) * 128, 128), 128)]
                    at = (half * 3 + c) * 64
                    fb[at : at + 64, t * 128 : (t + 1) * 128] = hot * tall(value[t : t + 1], 64)
        force[...] += dot_nt(fb[...], ohy[:, cols])
        return carry

    lax.fori_loop(0, 8, collect, 0)
    for h in halos:
        h.wait_send()
    for index, (src, dst) in enumerate(((req, asked), (rep, got), (outg, arrived))):
        some(src, dst, ND - 1, sent.at[index], reply_r).wait_send()


def finish(fo, motion, disp, base, force, fo_out, motion_out, disp_out, vel_out, disp_new, vel_new, sems):
    pairs = [(fo.at[i], fo_out.at[i]) for i in range(4)] + [(motion, motion_out), (disp_new, disp_out), (vel_new, vel_out)]
    copies = [pltpu.make_async_copy(a, b, sems.at[i]) for i, (a, b) in enumerate(pairs)]
    for c in copies[:5]:
        c.start()
    for c in range(3):
        total = force[c * 64 : (c + 1) * 64, :] + force[192 + c * 64 : 192 + (c + 1) * 64, :]
        for odd in range(2):
            rows = pl.ds(odd, 64, stride=2)
            vel = base[c, rows, :] + 0.3 * total[:, odd * 128 : (odd + 1) * 128]
            vel_new[c, rows, :] = vel
            disp_new[c, rows, :] = disp[c, rows, :] + 0.3 * vel
    for c in copies[5:]:
        c.start()
    for c in copies:
        c.wait()


def body(fluid, disp, vel, owners, nodes, weights, normals):
    small = pl.BlockSpec(memory_space=pltpu.VMEM)
    big = pl.BlockSpec(memory_space=pltpu.HBM)
    vm = pltpu.VMEM
    dma = pltpu.SemaphoreType.DMA
    scratch = [
        vm((4, CX + 6, CY, NZ), F32),
        vm((2, CX, CY + 16, NZ), F32),
        vm((2, PTS, NZ), F32),
        vm((3, 144, 128), F32),
        vm((3, 128, 128), F32),
        vm((ND, ENT), BF16),
        vm((K, PTS), I32),
        vm((CAP, ENT), BF16),
        vm((128, ENT), BF16),
        vm((1, ND, 128), F32),
        vm((1, ND, 128), F32),
        vm((CAP, 128), F32),
        vm((384, 512), BF16),
        vm((256, SLOTS), BF16),
        vm((64, SLOTS), BF16),
        vm((6, 8, 128), F32),
        vm((3, ND, 128), F32),
        vm((3, ND, 128), F32),
        vm((384, 256), BF16),
        vm((8, PTS), F32),
        vm((384, ENT), BF16),
        vm((2, ND, 128), F32),
        vm((2, ND, 128), F32),
        vm((384, 1024), BF16),
        vm((2, 8, 128), F32),
        vm((8, 128), F32),
        vm((8, 128), F32),
        dma((5,)),
        dma((8,)),
        dma((8,)),
        dma((3,)),
        dma((8,)),
        dma(()),
        dma((8,)),
    ]
    shapes = (fluid.shape, (6, PTS), disp.shape, vel.shape)
    kept = shapes + ((384, 256),)
    done = pl.pallas_call(
        kernel,
        name="coupling",
        out_shape=tuple(vm(shape, F32) for shape in kept),
        in_specs=[small] * 4 + [big] * 3,
        out_specs=(small,) * 5,
        scratch_shapes=scratch,
        compiler_params=pltpu.CompilerParams(
            collective_id=0, has_side_effects=True, vmem_limit_bytes=64_000_000
        ),
    )(owners.T, nodes.T, weights.T, normals, fluid, disp, vel)
    return pl.pallas_call(
        finish,
        name="finish",
        out_shape=tuple(jax.ShapeDtypeStruct(shape, F32) for shape in shapes),
        in_specs=[small] * 5,
        out_specs=(big,) * 4,
        scratch_shapes=[vm(disp.shape, F32), vm(vel.shape, F32), dma((7,))],
        compiler_params=pltpu.CompilerParams(vmem_limit_bytes=1024 * 1024),
    )(*[pltpu.with_memory_space_constraint(part, pltpu.VMEM) for part in done])


def solution(mesh):
    block, line = P(None, "span", "chord"), P(("span", "chord"), None)
    return jax.shard_map(
        body,
        mesh=mesh,
        in_specs=(P(None, "span", "chord", None), block, block, line, line, line, P(None, ("span", "chord"))),
        out_specs=(P(None, "span", "chord", None), P(None, ("span", "chord")), block, block),
        check_vma=False,
    )
```

```python
import jax
import jax.numpy as jnp
from jax import lax
from jax.experimental import pallas as pl
from jax.experimental.pallas import tpu as pltpu
from jax.sharding import PartitionSpec as P

MESH = pl.DeviceIdType.MESH
F32, BF16, I32 = jnp.float32, jnp.bfloat16, jnp.int32
NS, NC, ND = 16, 8, 128
CAP = 64
CX, CY, NZ = 32, 32, 128
PTS, K = 1024, 4
ENT = PTS * K
SLOTS = ND * CAP
QW = 256
SCALE = 0.4 / 60.0
NT = (((1,), (1,)), ((), ()))


def iota(shape, dim):
    return lax.broadcasted_iota(I32, shape, dim)


def split(value):
    high = value.astype(BF16)
    return high, (value - high.astype(F32)).astype(BF16)


def dot(a, b):
    return jnp.dot(a, b, preferred_element_type=F32)


def dot_nt(a, b):
    return lax.dot_general(a, b, NT, preferred_element_type=F32)


def diff(far_up, mid_up, up, down, mid_down, far_down):
    return 45.0 * (up - down) - 9.0 * (mid_up - mid_down) + (far_up - far_down)


def stencil(distance):
    size = jnp.abs(distance)
    value = jnp.where(size == 1, 45.0, jnp.where(size == 2, -9.0, jnp.where(size == 3, 1.0, 0.0)))
    return jnp.where(distance > 0, value, -value)


def kernel(
    own_ref, node_ref, w_ref, nrm_ref, fluid_hbm, disp_hbm, vel_hbm,
    fo, motion_ref, disp_ref, base_ref, force,
    xbuf, ybuf, pu, zb, dbuf, vbuf,
    onehot, rank, rankhot, reqb, req, asked, px,
    table, ohy, ohx, picked, rep, got, lookup, p0,
    loadb, outg, arrived, fb, colsend, collow, colhigh,
    in_sem, halo_s, halo_r, sent, ask_r, reply_r, load_r,
):
    span, chord = lax.axis_index("span"), lax.axis_index("chord")
    me = span * NC + chord

    xs, zs = span // 4, lax.rem(span, 4)
    mine = span // 2
    slot_row = mine * 8 + chord + 64 * lax.rem(span, 2)

    loads = [
        pltpu.make_async_copy(disp_hbm, dbuf.at[:, pl.ds(8, 128)], in_sem.at[0]),
        pltpu.make_async_copy(vel_hbm, vbuf, in_sem.at[1]),
        pltpu.make_async_copy(fluid_hbm.at[pl.ds(0, 2)], pu, in_sem.at[2]),
        pltpu.make_async_copy(fluid_hbm.at[pl.ds(2, 2)], xbuf.at[pl.ds(2, 2), pl.ds(3, CX)], in_sem.at[5]),
        pltpu.make_async_copy(fluid_hbm.at[0], ybuf.at[0, :, pl.ds(8, CY)], in_sem.at[3]),
        pltpu.make_async_copy(fluid_hbm.at[2], ybuf.at[1, :, pl.ds(8, CY)], in_sem.at[4]),
    ]
    for c in loads:
        c.start()

    barrier = pltpu.get_barrier_semaphore()

    def reach(k):
        return jnp.where(k == 0, 2, jnp.where(k == 3, 0, 2 * k - 1))

    def far_first(act):
        def one(k, carry):
            act(lax.rem(xs + reach(k // 4), 4) * 4 + lax.rem(zs + reach(lax.rem(k, 4)), 4))
            return carry

        lax.fori_loop(0, NS - 1, one, 0)

    def greet(s):
        for c in range(NC):
            pl.semaphore_signal(barrier, 1, device_id=(s, c), device_id_type=MESH)

    far_first(greet)
    for c in range(NC):

        @pl.when(c != chord)
        def _():
            pl.semaphore_signal(barrier, 1, device_id=(span, c), device_id_type=MESH)

    before = (iota((QW, QW), 0) < iota((QW, QW), 1)).astype(F32).astype(BF16)
    ones = jnp.ones((QW, QW), BF16)
    sub_o = iota((ND, QW), 0)
    sub_s = iota((CAP, QW), 0)
    offset = jnp.zeros((ND, QW), F32)
    for q in range(PTS // QW):
        cols = slice(q * QW, (q + 1) * QW)
        masks = []
        count = jnp.zeros((ND, QW), F32)
        for k in range(K):
            mask = sub_o == own_ref[k : k + 1, cols]
            masks.append(mask)
            hot = jnp.where(mask, 1.0, 0.0)
            onehot[:, k * PTS + q * QW : k * PTS + (q + 1) * QW] = hot.astype(BF16)
            count = count + hot
        count = count.astype(BF16)
        prior = dot(count, before) + offset
        offset = offset + dot(count, ones)
        for k in range(K):
            slot = jnp.sum(jnp.where(masks[k], prior, 0.0), axis=0, keepdims=True).astype(I32)
            node = node_ref[k : k + 1, cols]
            ent = slice(k * PTS + q * QW, k * PTS + (q + 1) * QW)
            at = sub_s == slot
            rankhot[:, ent] = jnp.where(at, 1.0, 0.0).astype(BF16)
            reqb[0:CAP, ent] = jnp.where(at, (node // 256).astype(F32), 0.0).astype(BF16)
            reqb[CAP:, ent] = jnp.where(at, lax.rem(node, 256).astype(F32), 0.0).astype(BF16)
            rank[k : k + 1, cols] = slot
    req[0] = dot_nt(onehot[...], reqb[...])

    for c in loads:
        c.wait()
    for c in range(6):
        for odd in range(2):
            value = dbuf[c, pl.ds(8 + odd, 64, stride=2), :] if c < 3 else vbuf[c - 3, pl.ds(odd, 64, stride=2), :]
            high, low = split(value)
            for t in range(4):
                rows = slice(t * 96 + c * 16, t * 96 + (c + 1) * 16)
                table[rows, odd * 128 : (odd + 1) * 128] = high[t * 16 : (t + 1) * 16]
                table[rows, 256 + odd * 128 : 256 + (odd + 1) * 128] = low[t * 16 : (t + 1) * 16]
    for c in range(3):
        turned = dbuf[c, 8:136, :].T
        colsend[0, c : c + 1, :] = turned[0:1, :]
        colsend[1, c : c + 1, :] = turned[127:128, :]
    force[...] = jnp.zeros((384, 256), F32)

    src, tgt = iota((NZ, NZ), 0), iota((NZ, NZ), 1)
    inner = stencil(src - tgt)
    ghost = jnp.where(src < 3, stencil(-(src + 1 + tgt)), 0.0)
    for i, tab in enumerate((inner + ghost, inner - ghost)):
        tab = tab.astype(BF16)
        tab = jnp.concatenate([tab, tab], axis=0)
        for b in range(4):
            value = pu[0, 8 * b : 8 * b + 8] if i == 0 else xbuf[3, 3 + 8 * b : 11 + 8 * b]
            high, low = split(value.reshape(256, NZ))
            zb[i, b * 256 : (b + 1) * 256, :] = dot(jnp.concatenate([high, low], axis=1), tab)

    def blend(x, carry):
        p, u = pu[0, x], pu[1, x]
        xbuf[0, x + 3] = 0.5 * p + u
        xbuf[1, x + 3] = 0.5 * u + p
        return carry

    lax.fori_loop(0, CX, blend, 0)

    pl.semaphore_wait(barrier, ND - 1)

    def row(ref, at):
        return ref.at[:, pl.ds(at, 1)]

    def redirect(s, c):
        own = (s == span) & (c == chord)
        return own, jnp.where(own, lax.rem(chord + 1, NC), c)

    def exchange(src, dst, index, recv):
        def send(s, c, row_at, to):
            pltpu.make_async_remote_copy(
                row(src, s * NC + c), row(dst, row_at), sent.at[index], recv.at[mine],
                device_id=(s, to), device_id_type=MESH,
            ).start()

        far_first(lambda s: [send(s, c, slot_row, c) for c in range(NC)])
        for c in range(NC):
            own, to = redirect(span, c)
            send(span, c, jnp.where(own, ND, slot_row), to)
        dst[:, pl.ds(slot_row, 1), :] = src[:, pl.ds(me, 1), :]

    def some(src, dst, count, send_sem, recv_sem):
        return pltpu.make_async_remote_copy(
            src.at[:, pl.ds(0, count)], dst.at[:, pl.ds(0, count)], send_sem, recv_sem,
            device_id=(span, chord), device_id_type=MESH,
        )

    def group_of(k):
        dx = jnp.where(k < 2, 0, jnp.where(k < 4, 2, jnp.where(lax.rem(k, 2) == 0, 1, 3)))
        dz = jnp.where(k < 2, k, jnp.where(k < 4, 3 - k, jnp.where(k < 6, 1, 0)))
        return lax.rem(xs + dx, 4) * 2 + lax.rem(zs // 2 + dz, 2)

    exchange(req, asked, 0, ask_r)

    up = (lax.rem(span + 1, NS), chord)
    down = (lax.rem(span + NS - 1, NS), chord)
    right = (span, lax.rem(chord + 1, NC))
    left = (span, lax.rem(chord + NC - 1, NC))
    moves = [
        (xbuf.at[0, pl.ds(CX, 3)], xbuf.at[0, pl.ds(0, 3)], up),
        (xbuf.at[0, pl.ds(3, 3)], xbuf.at[0, pl.ds(CX + 3, 3)], down),
        (ybuf.at[1, :, pl.ds(CY + 5, 3)], ybuf.at[1, :, pl.ds(5, 3)], right),
        (ybuf.at[1, :, pl.ds(8, 3)], ybuf.at[1, :, pl.ds(CY + 8, 3)], left),
        (xbuf.at[pl.ds(1, 3), pl.ds(CX, 3)], xbuf.at[pl.ds(1, 3), pl.ds(0, 3)], up),
        (xbuf.at[pl.ds(1, 3), pl.ds(3, 3)], xbuf.at[pl.ds(1, 3), pl.ds(CX + 3, 3)], down),
        (ybuf.at[0, :, pl.ds(CY + 5, 3)], ybuf.at[0, :, pl.ds(5, 3)], right),
        (ybuf.at[0, :, pl.ds(8, 3)], ybuf.at[0, :, pl.ds(CY + 8, 3)], left),
        (dbuf.at[:, pl.ds(135, 1)], dbuf.at[:, pl.ds(7, 1)], up),
        (dbuf.at[:, pl.ds(8, 1)], dbuf.at[:, pl.ds(136, 1)], down),
        (colsend.at[1], collow, right),
        (colsend.at[0], colhigh, left),
    ]
    halos = [
        pltpu.make_async_remote_copy(a, b, halo_s.at[i], halo_r.at[i], device_id=to, device_id_type=MESH)
        for i, (a, b, to) in enumerate(moves)
    ]
    for h in halos[:4]:
        h.start()

    lane8 = iota((8, 128), 1)
    sub8f = iota((8, QW), 0).astype(F32)
    low_y = iota((256, QW), 0).astype(F32).astype(BF16)
    low_x = iota((64, 128), 0).astype(F32).astype(BF16)
    one, zero = jnp.ones((), BF16), jnp.zeros((), BF16)

    def tall(line, rows):
        wide = jnp.broadcast_to(line, (16, line.shape[1])).astype(BF16)
        return jnp.concatenate([wide] * (rows // 16), axis=0)

    def hot_rows(numbers, line, rows):
        return jnp.where(numbers == tall(line, rows), one, zero)

    def halves(ref, j, g):
        low = ref[j, pl.ds(pl.multiple_of(g * 8, 8), 8), :]
        high = ref[j, pl.ds(pl.multiple_of(g * 8 + 64, 8), 8), :]
        front = jnp.where(lane8 < 64, low, pltpu.roll(high, 64, 1))
        back = jnp.where(lane8 < 64, pltpu.roll(low, 64, 1), high)
        return front, back

    def pick(k, g):
        xs_, ys_ = halves(asked, 0, g)
        px[k * 8 : (k + 1) * 8, :] = xs_
        for t in range(4):
            yrow = jnp.concatenate([ys_[2 * t : 2 * t + 1], ys_[2 * t + 1 : 2 * t + 2]], axis=1)
            ohy[:, (4 * k + t) * QW : (4 * k + t + 1) * QW] = hot_rows(low_y, yrow, 256)
        for t in range(4):
            xrow = jnp.concatenate([xs_[2 * t : 2 * t + 1], xs_[2 * t + 1 : 2 * t + 2]], axis=1)
            hot = ohy[:, (4 * k + t) * QW : (4 * k + t + 1) * QW]
            out = dot(table[...], jnp.concatenate([hot, hot], axis=0))
            sums = [jnp.zeros((8, QW), F32) for _ in range(6)]
            for i in range(8):
                mask = sub8f + 8.0 * i == xrow
                for c in range(6):
                    at = (i // 2) * 96 + c * 16 + (i % 2) * 8
                    sums[c] = sums[c] + jnp.where(mask, out[at : at + 8], 0.0)
            for c in range(6):
                line = jnp.sum(sums[c], axis=0, keepdims=True)
                picked[k % 2, c, 2 * t : 2 * t + 1, :] = line[:, 0:128]
                picked[k % 2, c, 2 * t + 1 : 2 * t + 2, :] = line[:, 128:256]
        for j in range(3):
            even, odd = picked[k % 2, 2 * j], picked[k % 2, 2 * j + 1]
            rep[j, k * 16 : k * 16 + 8, :] = jnp.where(lane8 < 64, even, pltpu.roll(odd, 64, 1))
            rep[j, k * 16 + 8 : k * 16 + 16, :] = jnp.where(lane8 < 64, pltpu.roll(even, 64, 1), odd)

    def reply(k, g):
        for half in range(2):
            for c in range(NC):
                to, at = c, me
                if k == 0:
                    own, to = redirect(2 * g + half, c)
                    at = jnp.where(own, ND, me)
                pltpu.make_async_remote_copy(
                    row(rep, k * 16 + 8 * half + c), row(got, at), sent.at[1], reply_r,
                    device_id=(2 * g + half, to), device_id_type=MESH,
                ).start()

    order = [group_of(k) for k in range(8)]
    for pair in range(4):
        for k in (2 * pair, 2 * pair + 1):
            some(req, asked, 16, sent.at[0], ask_r.at[order[k]]).wait_recv()
        if pair:
            reply(2 * pair - 2, order[2 * pair - 2])
            reply(2 * pair - 1, order[2 * pair - 1])
        pick(2 * pair, order[2 * pair])
        pick(2 * pair + 1, order[2 * pair + 1])
    reply(6, order[6])
    reply(7, order[7])
    got[:, pl.ds(me, 1), :] = rep[:, pl.ds(8 * lax.rem(span, 2) + chord, 1), :]

    for h in halos[4:]:
        h.start()

    def arrive(group, fields, yfield):
        for h in group:
            h.wait_recv()

        @pl.when(span == 0)
        def _():
            xbuf[fields, 0:3] = jnp.zeros((fields.stop - fields.start, 3, CY, NZ), F32)

        @pl.when(span == NS - 1)
        def _():
            xbuf[fields, CX + 3 : CX + 6] = jnp.zeros((fields.stop - fields.start, 3, CY, NZ), F32)

        @pl.when(chord == 0)
        def _():
            ybuf[yfield, :, 5:8, :] = jnp.zeros((CX, 3, NZ), F32)

        @pl.when(chord == NC - 1)
        def _():
            ybuf[yfield, :, CY + 8 : CY + 11, :] = jnp.zeros((CX, 3, NZ), F32)

    def dx(f, x):
        return diff(*[xbuf[f, x + 3 + o] for o in (3, 2, 1, -1, -2, -3)])

    def dy(f, x):
        return diff(*[ybuf[f, x, 8 + o : 8 + CY + o, :] for o in (3, 2, 1, -1, -2, -3)])

    def zrows(x):
        return pl.ds(pl.multiple_of(x * CY, CY), CY)

    def plane_p(x, carry):
        fo[0, x] = pu[0, x] - SCALE * (dx(0, x) + dy(1, x) + zb[1, zrows(x), :])
        return carry

    arrive(halos[:4], slice(0, 1), 1)
    lax.fori_loop(0, CX, plane_p, 0)
    for b in range(8):
        turned = fo[0, 4 * b : 4 * b + 4].reshape(128, NZ).T
        p0[0:1, b * 128 : (b + 1) * 128] = turned[0:1, :]

    def columns(g, carry):
        rows = pl.ds(pl.multiple_of(g * 8, 8), 8)
        places = px[rows, :]
        for t in range(8):
            ohx[:, pl.ds(pl.multiple_of((g * 8 + t) * 128, 128), 128)] = hot_rows(low_x, places[t : t + 1], 64)
        return carry

    lax.fori_loop(0, 8, columns, 0)

    some(rep, got, ND, sent.at[1], reply_r).wait_recv()
    for j in range(3):
        high, low = split(got[j, 0:ND].T)
        for c in range(2):
            for t in range(4):
                at = t * 96 + (2 * j + c) * 16
                lookup[at : at + 16, 0:128] = high[c * 64 + t * 16 : c * 64 + (t + 1) * 16]
                lookup[at : at + 16, 128:256] = low[c * 64 + t * 16 : c * 64 + (t + 1) * 16]

    sub8i = iota((8, QW), 0)

    def interp(q):
        cols = pl.ds(pl.multiple_of(q * QW, QW), QW)
        totals = [jnp.zeros((8, QW), F32) for _ in range(6)]
        for k in range(K):
            hot = onehot[:, pl.ds(pl.multiple_of(k * PTS + q * QW, QW), QW)]
            out = dot(lookup[...], jnp.concatenate([hot, hot], axis=0))
            slot = rank[k : k + 1, cols]
            weight = w_ref[k : k + 1, cols]
            sums = [jnp.zeros((8, QW), F32) for _ in range(6)]
            for i in range(8):
                mask = sub8i + 8 * i == slot
                for c in range(6):
                    at = (i // 2) * 96 + c * 16 + (i % 2) * 8
                    sums[c] = sums[c] + jnp.where(mask, out[at : at + 8], 0.0)
            for c in range(6):
                totals[c] = totals[c] + weight * sums[c]
        for c in range(6):
            motion_ref[c : c + 1, cols] = jnp.sum(totals[c], axis=0, keepdims=True)

    def interp_two(i, carry):
        interp(2 * i)
        interp(2 * i + 1)
        return carry

    lax.fori_loop(0, PTS // QW // 2, interp_two, 0)

    pressure = p0[0:1, :] + (SCALE * 74.0) * motion_ref[5:6, :]
    both = jnp.zeros((ND, 384), F32)
    push = [nrm_ref[c : c + 1, :] * pressure for c in range(3)]
    for k in range(K):
        ent = slice(k * PTS, (k + 1) * PTS)
        for c in range(3):
            value = push[c] * w_ref[k : k + 1, :]
            high = value.astype(BF16).astype(F32)
            for half, part in enumerate((high, value - high)):
                at = (c + 2 * half) * CAP if c < 2 else (4 + half) * CAP
                loadb[at : at + CAP, ent] = rankhot[:, ent] * tall(part, CAP)
        both = both + dot_nt(onehot[:, ent], loadb[:, ent])
    outg[0] = both[:, 0:128] + both[:, 128:256]
    outg[1] = both[:, 256:384] + pltpu.roll(both[:, 256:384], 64, 1)
    exchange(outg, arrived, 2, load_r)

    def plane_v(x, carry):
        fo[1, x] = pu[1, x] - SCALE * dx(1, x)
        fo[2, x] = xbuf[2, x + 3] - SCALE * (0.5 * dx(2, x) + dy(0, x))
        fo[3, x] = xbuf[3, x + 3] - SCALE * (0.5 * dx(3, x) + zb[0, zrows(x), :])
        return carry

    arrive(halos[4:], slice(1, 4), 0)

    @pl.when(span == 0)
    def _():
        dbuf[:, 7:8, :] = jnp.zeros((3, 1, 128), F32)

    @pl.when(span == NS - 1)
    def _():
        dbuf[:, 136:137, :] = jnp.zeros((3, 1, 128), F32)

    @pl.when(chord == 0)
    def _():
        collow[...] = jnp.zeros((8, 128), F32)

    @pl.when(chord == NC - 1)
    def _():
        colhigh[...] = jnp.zeros((8, 128), F32)

    lax.fori_loop(0, CX, plane_v, 0)

    zlane = iota((128, NZ), 1)
    reach = jnp.where(zlane == 0, 74.0 * SCALE, jnp.where(zlane == 1, -16.0 * SCALE, jnp.where(zlane == 2, 2.0 * SCALE, 0.0)))
    for b in range(8):
        turned = jnp.broadcast_to(motion_ref[5:6, b * 128 : (b + 1) * 128], (8, 128)).T
        fix = (turned[:, 0:1] * reach).reshape(4, CY, NZ)
        fo[0, 4 * b : 4 * b + 4] = fo[0, 4 * b : 4 * b + 4] + fix

    lane128 = iota((128, 128), 1)
    low_t, high_t = collow[...].T, colhigh[...].T
    for c in range(3):
        mid = dbuf[c, 8:136, :]
        west = jnp.where(lane128 == 0, low_t[:, c : c + 1], pltpu.roll(mid, 1, 1))
        east = jnp.where(lane128 == 127, high_t[:, c : c + 1], pltpu.roll(mid, 127, 1))
        lap = dbuf[c, 9:137, :] + dbuf[c, 7:135, :] + east + west - 4.0 * mid
        vel = vbuf[c]
        base_ref[c] = vel + 0.3 * (0.5 * lap - 0.2 * vel)
        disp_ref[c] = mid

    def collect(k, carry):
        k = jnp.where(k < 2, k, jnp.where(k < 4, k + 4, jnp.where(k < 6, k, 9 - k)))
        g = group_of(k)
        some(outg, arrived, 16, sent.at[2], load_r.at[g]).wait_recv()
        cols = pl.ds(pl.multiple_of(k * 1024, 1024), 1024)
        values = halves(arrived, 0, g) + halves(arrived, 1, g)[0:1]
        for c in range(3):
            high = values[c].astype(BF16).astype(F32)
            for half, value in enumerate((high, values[c] - high)):
                for t in range(8):
                    hot = ohx[:, pl.ds(pl.multiple_of((k * 8 + t) * 128, 128), 128)]
                    at = (half * 3 + c) * 64
                    fb[at : at + 64, t * 128 : (t + 1) * 128] = hot * tall(value[t : t + 1], 64)
        force[...] += dot_nt(fb[...], ohy[:, cols])
        return carry

    lax.fori_loop(0, 8, collect, 0)
    for h in halos:
        h.wait_send()
    for index, (src, dst) in enumerate(((req, asked), (rep, got), (outg, arrived))):
        some(src, dst, ND, sent.at[index], reply_r).wait_send()


def finish(fo, motion, disp, base, force, fo_out, motion_out, disp_out, vel_out, disp_new, vel_new, sems):
    pairs = [(fo.at[i], fo_out.at[i]) for i in range(4)] + [(motion, motion_out), (disp_new, disp_out), (vel_new, vel_out)]
    copies = [pltpu.make_async_copy(a, b, sems.at[i]) for i, (a, b) in enumerate(pairs)]
    for c in copies[:5]:
        c.start()
    for c in range(3):
        total = force[c * 64 : (c + 1) * 64, :] + force[192 + c * 64 : 192 + (c + 1) * 64, :]
        for odd in range(2):
            rows = pl.ds(odd, 64, stride=2)
            vel = base[c, rows, :] + 0.3 * total[:, odd * 128 : (odd + 1) * 128]
            vel_new[c, rows, :] = vel
            disp_new[c, rows, :] = disp[c, rows, :] + 0.3 * vel
    for c in copies[5:]:
        c.start()
    for c in copies:
        c.wait()


def body(fluid, disp, vel, owners, nodes, weights, normals):
    small = pl.BlockSpec(memory_space=pltpu.VMEM)
    big = pl.BlockSpec(memory_space=pltpu.HBM)
    vm = pltpu.VMEM
    dma = pltpu.SemaphoreType.DMA
    scratch = [
        vm((4, CX + 6, CY, NZ), F32),
        vm((2, CX, CY + 16, NZ), F32),
        vm((2, CX, CY, NZ), F32),
        vm((2, PTS, NZ), F32),
        vm((3, 144, 128), F32),
        vm((3, 128, 128), F32),
        vm((ND, ENT), BF16),
        vm((K, PTS), I32),
        vm((CAP, ENT), BF16),
        vm((128, ENT), BF16),
        vm((1, ND, 128), F32),
        vm((1, ND + 8, 128), F32),
        vm((CAP, 128), F32),
        vm((384, 512), BF16),
        vm((256, SLOTS), BF16),
        vm((64, SLOTS), BF16),
        vm((2, 6, 8, 128), F32),
        vm((3, ND, 128), F32),
        vm((3, ND + 8, 128), F32),
        vm((384, 256), BF16),
        vm((8, PTS), F32),
        vm((384, ENT), BF16),
        vm((2, ND, 128), F32),
        vm((2, ND + 8, 128), F32),
        vm((384, 1024), BF16),
        vm((2, 8, 128), F32),
        vm((8, 128), F32),
        vm((8, 128), F32),
        dma((6,)),
        dma((12,)),
        dma((12,)),
        dma((3,)),
        dma((8,)),
        dma(()),
        dma((8,)),
    ]
    shapes = (fluid.shape, (6, PTS), disp.shape, vel.shape)
    kept = shapes + ((384, 256),)
    done = pl.pallas_call(
        kernel,
        name="coupling",
        out_shape=tuple(vm(shape, F32) for shape in kept),
        in_specs=[small] * 4 + [big] * 3,
        out_specs=(small,) * 5,
        scratch_shapes=scratch,
        compiler_params=pltpu.CompilerParams(
            collective_id=0, has_side_effects=True, vmem_limit_bytes=64_000_000
        ),
    )(owners.T, nodes.T, weights.T, normals, fluid, disp, vel)
    return pl.pallas_call(
        finish,
        name="finish",
        out_shape=tuple(jax.ShapeDtypeStruct(shape, F32) for shape in shapes),
        in_specs=[small] * 5,
        out_specs=(big,) * 4,
        scratch_shapes=[vm(disp.shape, F32), vm(vel.shape, F32), dma((7,))],
        compiler_params=pltpu.CompilerParams(vmem_limit_bytes=1024 * 1024),
    )(*[pltpu.with_memory_space_constraint(part, pltpu.VMEM) for part in done])


def solution(mesh):
    block, line = P(None, "span", "chord"), P(("span", "chord"), None)
    return jax.shard_map(
        body,
        mesh=mesh,
        in_specs=(P(None, "span", "chord", None), block, block, line, line, line, P(None, ("span", "chord"))),
        out_specs=(P(None, "span", "chord", None), P(None, ("span", "chord")), block, block),
        check_vma=False,
    )
```

```python
import jax
import jax.numpy as jnp
from jax import lax
from jax.experimental import pallas as pl
from jax.experimental.pallas import tpu as pltpu
from jax.sharding import PartitionSpec as P

MESH = pl.DeviceIdType.MESH
F32, BF16, I32 = jnp.float32, jnp.bfloat16, jnp.int32
NS, NC, ND = 16, 8, 128
CAP = 64
CX, CY, NZ = 32, 32, 128
PTS, K = 1024, 4
ENT = PTS * K
SLOTS = ND * CAP
QW = 256
SCALE = 0.4 / 60.0
NT = (((1,), (1,)), ((), ()))


def iota(shape, dim):
    return lax.broadcasted_iota(I32, shape, dim)


def split(value):
    high = value.astype(BF16)
    return high, (value - high.astype(F32)).astype(BF16)


def dot(a, b):
    return jnp.dot(a, b, preferred_element_type=F32)


def dot_nt(a, b):
    return lax.dot_general(a, b, NT, preferred_element_type=F32)


def diff(far_up, mid_up, up, down, mid_down, far_down):
    return 45.0 * (up - down) - 9.0 * (mid_up - mid_down) + (far_up - far_down)


def stencil(distance):
    size = jnp.abs(distance)
    value = jnp.where(size == 1, 45.0, jnp.where(size == 2, -9.0, jnp.where(size == 3, 1.0, 0.0)))
    return jnp.where(distance > 0, value, -value)


def tall(line, rows):
    wide = jnp.broadcast_to(line, (16, line.shape[1])).astype(BF16)
    return jnp.concatenate([wide] * (rows // 16), axis=0)


EARLY, LATE = ((0, 1),), (6, 7, 4, 5, 3, 2)


def weigh(part, ready, ohx, ohy, fb):
    for i, k in enumerate(part):
        for c in range(3):
            high = ready[i][c].astype(BF16).astype(F32)
            for half, value in enumerate((high, ready[i][c] - high)):
                for t in range(8):
                    hot = ohx[:, (k * 8 + t) * 128 : (k * 8 + t + 1) * 128]
                    at = (half * 3 + c) * 64
                    fb[at : at + 64, i * 1024 + t * 128 : i * 1024 + (t + 1) * 128] = hot * tall(value[t : t + 1], 64)
    total = jnp.zeros((384, 256), F32)
    for i, k in enumerate(part):
        total = total + dot_nt(fb[:, i * 1024 : (i + 1) * 1024], ohy[:, k * 1024 : (k + 1) * 1024])
    return total


def kernel(
    own_ref, node_ref, w_ref, nrm_ref, fluid_hbm, disp_hbm, vel_hbm,
    fo, motion_ref, disp_ref, base_ref, force, late, ohx, ohy,
    xbuf, ybuf, pu, zb, dbuf, vbuf,
    onehot, rank, rankhot, reqb, req, asked, px,
    table, picked, rep, got, lookup, p0,
    loadb, outg, arrived, fb, colsend, collow, colhigh,
    in_sem, halo_s, halo_r, sent, ask_r, reply_r, load_r,
):
    span, chord = lax.axis_index("span"), lax.axis_index("chord")
    me = span * NC + chord

    xs, zs = span // 4, lax.rem(span, 4)
    mine = span // 2
    slot_row = mine * 8 + chord + 64 * lax.rem(span, 2)

    loads = [
        pltpu.make_async_copy(disp_hbm, dbuf.at[:, pl.ds(8, 128)], in_sem.at[0]),
        pltpu.make_async_copy(vel_hbm, vbuf, in_sem.at[1]),
        pltpu.make_async_copy(fluid_hbm.at[pl.ds(0, 2)], pu, in_sem.at[2]),
        pltpu.make_async_copy(fluid_hbm.at[pl.ds(2, 2)], xbuf.at[pl.ds(2, 2), pl.ds(3, CX)], in_sem.at[5]),
        pltpu.make_async_copy(fluid_hbm.at[0], ybuf.at[0, :, pl.ds(8, CY)], in_sem.at[3]),
        pltpu.make_async_copy(fluid_hbm.at[2], ybuf.at[1, :, pl.ds(8, CY)], in_sem.at[4]),
    ]
    for c in loads:
        c.start()

    barrier = pltpu.get_barrier_semaphore()

    def reach(k):
        return jnp.where(k == 0, 2, jnp.where(k == 3, 0, 2 * k - 1))

    def far_first(act):
        def one(k, carry):
            act(lax.rem(xs + reach(k // 4), 4) * 4 + lax.rem(zs + reach(lax.rem(k, 4)), 4))
            return carry

        lax.fori_loop(0, NS - 1, one, 0)

    def greet(s):
        for c in range(NC):
            pl.semaphore_signal(barrier, 1, device_id=(s, c), device_id_type=MESH)

    far_first(greet)
    for c in range(NC):

        @pl.when(c != chord)
        def _():
            pl.semaphore_signal(barrier, 1, device_id=(span, c), device_id_type=MESH)

    before = (iota((QW, QW), 0) < iota((QW, QW), 1)).astype(F32).astype(BF16)
    ones = jnp.ones((QW, QW), BF16)
    sub_o = iota((ND, QW), 0)
    sub_s = iota((CAP, QW), 0)
    offset = jnp.zeros((ND, QW), F32)
    for q in range(PTS // QW):
        cols = slice(q * QW, (q + 1) * QW)
        masks = []
        count = jnp.zeros((ND, QW), F32)
        for k in range(K):
            mask = sub_o == own_ref[k : k + 1, cols]
            masks.append(mask)
            hot = jnp.where(mask, 1.0, 0.0)
            onehot[:, k * PTS + q * QW : k * PTS + (q + 1) * QW] = hot.astype(BF16)
            count = count + hot
        count = count.astype(BF16)
        prior = dot(count, before) + offset
        offset = offset + dot(count, ones)
        for k in range(K):
            slot = jnp.sum(jnp.where(masks[k], prior, 0.0), axis=0, keepdims=True).astype(I32)
            node = node_ref[k : k + 1, cols]
            ent = slice(k * PTS + q * QW, k * PTS + (q + 1) * QW)
            at = sub_s == slot
            rankhot[:, ent] = jnp.where(at, 1.0, 0.0).astype(BF16)
            reqb[0:CAP, ent] = jnp.where(at, (node // 256).astype(F32), 0.0).astype(BF16)
            reqb[CAP:, ent] = jnp.where(at, lax.rem(node, 256).astype(F32), 0.0).astype(BF16)
            rank[k : k + 1, cols] = slot
    req[0] = dot_nt(onehot[...], reqb[...])

    for c in loads:
        c.wait()
    for c in range(6):
        for odd in range(2):
            value = dbuf[c, pl.ds(8 + odd, 64, stride=2), :] if c < 3 else vbuf[c - 3, pl.ds(odd, 64, stride=2), :]
            high, low = split(value)
            for t in range(4):
                rows = slice(t * 96 + c * 16, t * 96 + (c + 1) * 16)
                table[rows, odd * 128 : (odd + 1) * 128] = high[t * 16 : (t + 1) * 16]
                table[rows, 256 + odd * 128 : 256 + (odd + 1) * 128] = low[t * 16 : (t + 1) * 16]
    for c in range(3):
        turned = dbuf[c, 8:136, :].T
        colsend[0, c : c + 1, :] = turned[0:1, :]
        colsend[1, c : c + 1, :] = turned[127:128, :]

    src, tgt = iota((NZ, NZ), 0), iota((NZ, NZ), 1)
    inner = stencil(src - tgt)
    ghost = jnp.where(src < 3, stencil(-(src + 1 + tgt)), 0.0)
    for i, tab in enumerate((inner + ghost, inner - ghost)):
        tab = tab.astype(BF16)
        tab = jnp.concatenate([tab, tab], axis=0)
        for b in range(4):
            value = pu[0, 8 * b : 8 * b + 8] if i == 0 else xbuf[3, 3 + 8 * b : 11 + 8 * b]
            high, low = split(value.reshape(256, NZ))
            zb[i, b * 256 : (b + 1) * 256, :] = dot(jnp.concatenate([high, low], axis=1), tab)

    def blend(x, carry):
        p, u = pu[0, x], pu[1, x]
        xbuf[0, x + 3] = 0.5 * p + u
        xbuf[1, x + 3] = 0.5 * u + p
        return carry

    lax.fori_loop(0, CX, blend, 0)

    pl.semaphore_wait(barrier, ND - 1)

    def row(ref, at):
        return ref.at[:, pl.ds(at, 1)]

    def redirect(s, c):
        own = (s == span) & (c == chord)
        return own, jnp.where(own, lax.rem(chord + 1, NC), c)

    def exchange(src, dst, index, recv):
        def send(s, c, row_at, to):
            pltpu.make_async_remote_copy(
                row(src, s * NC + c), row(dst, row_at), sent.at[index], recv.at[mine],
                device_id=(s, to), device_id_type=MESH,
            ).start()

        far_first(lambda s: [send(s, c, slot_row, c) for c in range(NC)])
        for c in range(NC):
            own, to = redirect(span, c)
            send(span, c, jnp.where(own, ND, slot_row), to)
        dst[:, pl.ds(slot_row, 1), :] = src[:, pl.ds(me, 1), :]

    def some(src, dst, count, send_sem, recv_sem):
        return pltpu.make_async_remote_copy(
            src.at[:, pl.ds(0, count)], dst.at[:, pl.ds(0, count)], send_sem, recv_sem,
            device_id=(span, chord), device_id_type=MESH,
        )

    def group_of(k):
        dx = jnp.where(k < 2, 0, jnp.where(k < 4, 2, jnp.where(lax.rem(k, 2) == 0, 1, 3)))
        dz = jnp.where(k < 2, k, jnp.where(k < 4, 3 - k, jnp.where(k < 6, 1, 0)))
        return lax.rem(xs + dx, 4) * 2 + lax.rem(zs // 2 + dz, 2)

    exchange(req, asked, 0, ask_r)

    up = (lax.rem(span + 1, NS), chord)
    down = (lax.rem(span + NS - 1, NS), chord)
    right = (span, lax.rem(chord + 1, NC))
    left = (span, lax.rem(chord + NC - 1, NC))
    moves = [
        (xbuf.at[0, pl.ds(CX, 3)], xbuf.at[0, pl.ds(0, 3)], up),
        (xbuf.at[0, pl.ds(3, 3)], xbuf.at[0, pl.ds(CX + 3, 3)], down),
        (ybuf.at[1, :, pl.ds(CY + 5, 3)], ybuf.at[1, :, pl.ds(5, 3)], right),
        (ybuf.at[1, :, pl.ds(8, 3)], ybuf.at[1, :, pl.ds(CY + 8, 3)], left),
        (xbuf.at[pl.ds(1, 3), pl.ds(CX, 3)], xbuf.at[pl.ds(1, 3), pl.ds(0, 3)], up),
        (xbuf.at[pl.ds(1, 3), pl.ds(3, 3)], xbuf.at[pl.ds(1, 3), pl.ds(CX + 3, 3)], down),
        (ybuf.at[0, :, pl.ds(CY + 5, 3)], ybuf.at[0, :, pl.ds(5, 3)], right),
        (ybuf.at[0, :, pl.ds(8, 3)], ybuf.at[0, :, pl.ds(CY + 8, 3)], left),
        (dbuf.at[:, pl.ds(135, 1)], dbuf.at[:, pl.ds(7, 1)], up),
        (dbuf.at[:, pl.ds(8, 1)], dbuf.at[:, pl.ds(136, 1)], down),
        (colsend.at[1], collow, right),
        (colsend.at[0], colhigh, left),
    ]
    halos = [
        pltpu.make_async_remote_copy(a, b, halo_s.at[i], halo_r.at[i], device_id=to, device_id_type=MESH)
        for i, (a, b, to) in enumerate(moves)
    ]
    for h in halos:
        h.start()

    lane8 = iota((8, 128), 1)
    sub8f = iota((8, QW), 0).astype(F32)
    low_y = iota((256, QW), 0).astype(F32).astype(BF16)
    low_x = iota((64, 128), 0).astype(F32).astype(BF16)
    one, zero = jnp.ones((), BF16), jnp.zeros((), BF16)

    def hot_rows(numbers, line, rows):
        return jnp.where(numbers == tall(line, rows), one, zero)

    def halves(ref, j, g):
        low = ref[j, pl.ds(pl.multiple_of(g * 8, 8), 8), :]
        high = ref[j, pl.ds(pl.multiple_of(g * 8 + 64, 8), 8), :]
        front = jnp.where(lane8 < 64, low, pltpu.roll(high, 64, 1))
        back = jnp.where(lane8 < 64, pltpu.roll(low, 64, 1), high)
        return front, back

    def pick(k, g):
        xs_, ys_ = halves(asked, 0, g)
        px[k * 8 : (k + 1) * 8, :] = xs_
        for t in range(4):
            yrow = jnp.concatenate([ys_[2 * t : 2 * t + 1], ys_[2 * t + 1 : 2 * t + 2]], axis=1)
            ohy[:, (4 * k + t) * QW : (4 * k + t + 1) * QW] = hot_rows(low_y, yrow, 256)
        for t in range(4):
            xrow = jnp.concatenate([xs_[2 * t : 2 * t + 1], xs_[2 * t + 1 : 2 * t + 2]], axis=1)
            hot = ohy[:, (4 * k + t) * QW : (4 * k + t + 1) * QW]
            out = dot(table[...], jnp.concatenate([hot, hot], axis=0))
            sums = [jnp.zeros((8, QW), F32) for _ in range(6)]
            for i in range(8):
                mask = sub8f + 8.0 * i == xrow
                for c in range(6):
                    at = (i // 2) * 96 + c * 16 + (i % 2) * 8
                    sums[c] = sums[c] + jnp.where(mask, out[at : at + 8], 0.0)
            for c in range(6):
                line = jnp.sum(sums[c], axis=0, keepdims=True)
                picked[k % 2, c, 2 * t : 2 * t + 1, :] = line[:, 0:128]
                picked[k % 2, c, 2 * t + 1 : 2 * t + 2, :] = line[:, 128:256]
        for j in range(3):
            even, odd = picked[k % 2, 2 * j], picked[k % 2, 2 * j + 1]
            rep[j, k * 16 : k * 16 + 8, :] = jnp.where(lane8 < 64, even, pltpu.roll(odd, 64, 1))
            rep[j, k * 16 + 8 : k * 16 + 16, :] = jnp.where(lane8 < 64, pltpu.roll(even, 64, 1), odd)

    def reply(k, g):
        for half in range(2):
            for c in range(NC):
                to, at = c, me
                if k == 0:
                    own, to = redirect(2 * g + half, c)
                    at = jnp.where(own, ND, me)
                pltpu.make_async_remote_copy(
                    row(rep, k * 16 + 8 * half + c), row(got, at), sent.at[1], reply_r,
                    device_id=(2 * g + half, to), device_id_type=MESH,
                ).start()

    order = [group_of(k) for k in range(8)]
    for pair in range(4):
        for k in (2 * pair, 2 * pair + 1):
            some(req, asked, 16, sent.at[0], ask_r.at[order[k]]).wait_recv()
        pick(2 * pair, order[2 * pair])
        pick(2 * pair + 1, order[2 * pair + 1])
        reply(2 * pair, order[2 * pair])
        reply(2 * pair + 1, order[2 * pair + 1])
    got[:, pl.ds(me, 1), :] = rep[:, pl.ds(8 * lax.rem(span, 2) + chord, 1), :]

    def arrive(group, fields, yfield):
        for h in group:
            h.wait_recv()

        @pl.when(span == 0)
        def _():
            xbuf[fields, 0:3] = jnp.zeros((fields.stop - fields.start, 3, CY, NZ), F32)

        @pl.when(span == NS - 1)
        def _():
            xbuf[fields, CX + 3 : CX + 6] = jnp.zeros((fields.stop - fields.start, 3, CY, NZ), F32)

        @pl.when(chord == 0)
        def _():
            ybuf[yfield, :, 5:8, :] = jnp.zeros((CX, 3, NZ), F32)

        @pl.when(chord == NC - 1)
        def _():
            ybuf[yfield, :, CY + 8 : CY + 11, :] = jnp.zeros((CX, 3, NZ), F32)

    def dx(f, x):
        return diff(*[xbuf[f, x + 3 + o] for o in (3, 2, 1, -1, -2, -3)])

    def dy(f, x):
        return diff(*[ybuf[f, x, 8 + o : 8 + CY + o, :] for o in (3, 2, 1, -1, -2, -3)])

    def zrows(x):
        return pl.ds(pl.multiple_of(x * CY, CY), CY)

    def plane_p(x, carry):
        fo[0, x] = pu[0, x] - SCALE * (dx(0, x) + dy(1, x) + zb[1, zrows(x), :])
        return carry

    arrive(halos[:4], slice(0, 1), 1)
    lax.fori_loop(0, CX, plane_p, 0)
    for b in range(8):
        turned = fo[0, 4 * b : 4 * b + 4].reshape(128, NZ).T
        p0[0:1, b * 128 : (b + 1) * 128] = turned[0:1, :]

    def columns(g, carry):
        rows = pl.ds(pl.multiple_of(g * 8, 8), 8)
        places = px[rows, :]
        for t in range(8):
            ohx[:, pl.ds(pl.multiple_of((g * 8 + t) * 128, 128), 128)] = hot_rows(low_x, places[t : t + 1], 64)
        return carry

    lax.fori_loop(0, 8, columns, 0)

    def plane_v(x, carry):
        fo[1, x] = pu[1, x] - SCALE * dx(1, x)
        fo[2, x] = xbuf[2, x + 3] - SCALE * (0.5 * dx(2, x) + dy(0, x))
        fo[3, x] = xbuf[3, x + 3] - SCALE * (0.5 * dx(3, x) + zb[0, zrows(x), :])
        return carry

    arrive(halos[4:], slice(1, 4), 0)

    @pl.when(span == 0)
    def _():
        dbuf[:, 7:8, :] = jnp.zeros((3, 1, 128), F32)

    @pl.when(span == NS - 1)
    def _():
        dbuf[:, 136:137, :] = jnp.zeros((3, 1, 128), F32)

    @pl.when(chord == 0)
    def _():
        collow[...] = jnp.zeros((8, 128), F32)

    @pl.when(chord == NC - 1)
    def _():
        colhigh[...] = jnp.zeros((8, 128), F32)

    lax.fori_loop(0, CX, plane_v, 0)

    lane128 = iota((128, 128), 1)
    low_t, high_t = collow[...].T, colhigh[...].T
    for c in range(3):
        mid = dbuf[c, 8:136, :]
        west = jnp.where(lane128 == 0, low_t[:, c : c + 1], pltpu.roll(mid, 1, 1))
        east = jnp.where(lane128 == 127, high_t[:, c : c + 1], pltpu.roll(mid, 127, 1))
        lap = dbuf[c, 9:137, :] + dbuf[c, 7:135, :] + east + west - 4.0 * mid
        vel = vbuf[c]
        base_ref[c] = vel + 0.3 * (0.5 * lap - 0.2 * vel)
        disp_ref[c] = mid

    some(rep, got, ND, sent.at[1], reply_r).wait_recv()
    for j in range(3):
        high, low = split(got[j, 0:ND].T)
        for c in range(2):
            for t in range(4):
                at = t * 96 + (2 * j + c) * 16
                lookup[at : at + 16, 0:128] = high[c * 64 + t * 16 : c * 64 + (t + 1) * 16]
                lookup[at : at + 16, 128:256] = low[c * 64 + t * 16 : c * 64 + (t + 1) * 16]

    sub8i = iota((8, QW), 0)

    def interp(q):
        cols = pl.ds(pl.multiple_of(q * QW, QW), QW)
        totals = [jnp.zeros((8, QW), F32) for _ in range(6)]
        for k in range(K):
            hot = onehot[:, pl.ds(pl.multiple_of(k * PTS + q * QW, QW), QW)]
            out = dot(lookup[...], jnp.concatenate([hot, hot], axis=0))
            slot = rank[k : k + 1, cols]
            weight = w_ref[k : k + 1, cols]
            sums = [jnp.zeros((8, QW), F32) for _ in range(6)]
            for i in range(8):
                mask = sub8i + 8 * i == slot
                for c in range(6):
                    at = (i // 2) * 96 + c * 16 + (i % 2) * 8
                    sums[c] = sums[c] + jnp.where(mask, out[at : at + 8], 0.0)
            for c in range(6):
                totals[c] = totals[c] + weight * sums[c]
        for c in range(6):
            motion_ref[c : c + 1, cols] = jnp.sum(totals[c], axis=0, keepdims=True)

    def interp_two(i, carry):
        interp(2 * i)
        interp(2 * i + 1)
        return carry

    lax.fori_loop(0, PTS // QW // 2, interp_two, 0)

    pressure = p0[0:1, :] + (SCALE * 74.0) * motion_ref[5:6, :]
    both = jnp.zeros((ND, 384), F32)
    push = [nrm_ref[c : c + 1, :] * pressure for c in range(3)]
    for k in range(K):
        ent = slice(k * PTS, (k + 1) * PTS)
        for c in range(3):
            value = push[c] * w_ref[k : k + 1, :]
            high = value.astype(BF16).astype(F32)
            for half, part in enumerate((high, value - high)):
                at = (c + 2 * half) * CAP if c < 2 else (4 + half) * CAP
                loadb[at : at + CAP, ent] = rankhot[:, ent] * tall(part, CAP)
        both = both + dot_nt(onehot[:, ent], loadb[:, ent])
    outg[0] = both[:, 0:128] + both[:, 128:256]
    outg[1] = both[:, 256:384] + pltpu.roll(both[:, 256:384], 64, 1)
    exchange(outg, arrived, 2, load_r)

    zlane = iota((128, NZ), 1)
    reach = jnp.where(zlane == 0, 74.0 * SCALE, jnp.where(zlane == 1, -16.0 * SCALE, jnp.where(zlane == 2, 2.0 * SCALE, 0.0)))
    for b in range(8):
        turned = jnp.broadcast_to(motion_ref[5:6, b * 128 : (b + 1) * 128], (8, 128)).T
        fix = (turned[:, 0:1] * reach).reshape(4, CY, NZ)
        fo[0, 4 * b : 4 * b + 4] = fo[0, 4 * b : 4 * b + 4] + fix

    def loads_of(k):
        g = order[k]
        some(outg, arrived, 16, sent.at[2], load_r.at[g]).wait_recv()
        return halves(arrived, 0, g) + halves(arrived, 1, g)[0:1]

    for index, part in enumerate(EARLY):
        ready = [loads_of(k) for k in part]
        total = weigh(part, ready, ohx, ohy, fb)
        force[...] = total if index == 0 else force[...] + total
    for i, k in enumerate(LATE):
        for c, value in enumerate(loads_of(k)):
            late[3 * i + c] = value

    for h in halos:
        h.wait_send()
    for index, (src, dst) in enumerate(((req, asked), (rep, got), (outg, arrived))):
        some(src, dst, ND, sent.at[index], reply_r).wait_send()


def finish(
    fo, motion, disp, base, force, late, ohx, ohy,
    fo_out, motion_out, disp_out, vel_out,
    disp_new, vel_new, fb, sems,
):
    pairs = [(fo.at[i], fo_out.at[i]) for i in range(4)] + [(motion, motion_out), (disp_new, disp_out), (vel_new, vel_out)]
    copies = [pltpu.make_async_copy(a, b, sems.at[i]) for i, (a, b) in enumerate(pairs)]
    for c in copies[:5]:
        c.start()
    sums = force[...] + weigh(LATE, [[late[3 * i + c] for c in range(3)] for i in range(len(LATE))], ohx, ohy, fb)
    for c in range(3):
        total = sums[c * 64 : (c + 1) * 64, :] + sums[192 + c * 64 : 192 + (c + 1) * 64, :]
        for odd in range(2):
            rows = pl.ds(odd, 64, stride=2)
            vel = base[c, rows, :] + 0.3 * total[:, odd * 128 : (odd + 1) * 128]
            vel_new[c, rows, :] = vel
            disp_new[c, rows, :] = disp[c, rows, :] + 0.3 * vel
    for c in copies[5:]:
        c.start()
    for c in copies:
        c.wait()


def body(fluid, disp, vel, owners, nodes, weights, normals):
    small = pl.BlockSpec(memory_space=pltpu.VMEM)
    big = pl.BlockSpec(memory_space=pltpu.HBM)
    vm = pltpu.VMEM
    dma = pltpu.SemaphoreType.DMA
    scratch = [
        vm((4, CX + 6, CY, NZ), F32),
        vm((2, CX, CY + 16, NZ), F32),
        vm((2, CX, CY, NZ), F32),
        vm((2, PTS, NZ), F32),
        vm((3, 144, 128), F32),
        vm((3, 128, 128), F32),
        vm((ND, ENT), BF16),
        vm((K, PTS), I32),
        vm((CAP, ENT), BF16),
        vm((128, ENT), BF16),
        vm((1, ND, 128), F32),
        vm((1, ND + 8, 128), F32),
        vm((CAP, 128), F32),
        vm((384, 512), BF16),
        vm((2, 6, 8, 128), F32),
        vm((3, ND, 128), F32),
        vm((3, ND + 8, 128), F32),
        vm((384, 256), BF16),
        vm((8, PTS), F32),
        vm((384, ENT), BF16),
        vm((2, ND, 128), F32),
        vm((2, ND + 8, 128), F32),
        vm((384, 2048), BF16),
        vm((2, 8, 128), F32),
        vm((8, 128), F32),
        vm((8, 128), F32),
        dma((6,)),
        dma((12,)),
        dma((12,)),
        dma((3,)),
        dma((8,)),
        dma(()),
        dma((8,)),
    ]
    shapes = (fluid.shape, (6, PTS), disp.shape, vel.shape)
    kept = [vm(shape, F32) for shape in shapes + ((384, 256), (3 * len(LATE), 8, 128))]
    kept += [vm((64, SLOTS), BF16), vm((256, SLOTS), BF16)]
    done = pl.pallas_call(
        kernel,
        name="coupling",
        out_shape=tuple(kept),
        in_specs=[small] * 4 + [big] * 3,
        out_specs=(small,) * 8,
        scratch_shapes=scratch,
        compiler_params=pltpu.CompilerParams(
            collective_id=0, has_side_effects=True, vmem_limit_bytes=58_400_000
        ),
    )(owners.T, nodes.T, weights.T, normals, fluid, disp, vel)
    return pl.pallas_call(
        finish,
        name="finish",
        out_shape=tuple(jax.ShapeDtypeStruct(shape, F32) for shape in shapes),
        in_specs=[small] * 8,
        out_specs=(big,) * 4,
        scratch_shapes=[vm(disp.shape, F32), vm(vel.shape, F32), vm((384, 1024 * len(LATE)), BF16), dma((7,))],
        compiler_params=pltpu.CompilerParams(vmem_limit_bytes=6 * 1024 * 1024),
    )(*[pltpu.with_memory_space_constraint(part, pltpu.VMEM) for part in done])


def solution(mesh):
    block, line = P(None, "span", "chord"), P(("span", "chord"), None)
    return jax.shard_map(
        body,
        mesh=mesh,
        in_specs=(P(None, "span", "chord", None), block, block, line, line, line, P(None, ("span", "chord"))),
        out_specs=(P(None, "span", "chord", None), P(None, ("span", "chord")), block, block),
        check_vma=False,
    )
```
